32 devices in a mesh: src: 4 (over x, core), rcv: 8 (over z, y).
Axes of the slice: x: 2, y: 2, z: 4, core: 2. Of those that a mesh axis runs over, the one named last changes fastest.
Arguments:
- wavefield: bfloat16 [1024, 1024, 256], P('src', 'rcv'), may hold values from -6 to 6
- inverse_wavelet: float32 [2, 64], replicated, may hold values from -0.05 to 0.05
Outputs:
- primaries: bfloat16 [1024, 1024, 256], P('src', 'rcv')
The draws below stay inside these ranges and needn't reach their ends.
All inputs are finite; a program needn't handle non-finite values.
Results may differ from the reference program's by a relative error of at most 0.0091.
Values may be sent and summed in bfloat16 or wider, within the bound.
No kernel may reach another device: no remote copies, remote signals or barrier semaphores. Data moves between devices by JAX's collectives and lax.ppermute only.
A program may use at most 256 MiB of HBM per device.

```python
import math
import jax
import jax.numpy as jnp
from jax import lax

NS = 1024
NT = 256
F = 64
F0 = 8


def shard_levels(key, shape, shards, low, largest):
    level = 1.0
    for position, parts in shards:
        heights = jax.random.uniform(jax.random.fold_in(jax.random.fold_in(key, 6), position), (parts,), jnp.float32, low / len(shards), largest / len(shards))
        level = level * jnp.repeat(jnp.exp(heights), shape[position] // parts).reshape((-1,) + (1,) * (len(shape) - 1 - position))
    return level


def scatter_about(stream_key, shape, deviation, most, split=(), kind=jnp.bfloat16):
    gain = shard_levels(stream_key, shape, split, -0.22, 0.18) if split else 1.0
    drawn = jax.random.normal(stream_key, shape, jnp.float32) * deviation * gain
    return jnp.minimum(jnp.maximum(drawn, -most), most).astype(kind)


def setup_inputs(seed: int = 0) -> dict:
    arg_keys = jax.random.split(jax.random.key(seed), 3)
    wavefield = scatter_about(arg_keys[0], (NS, NS, NT), 1.0, 6.0, ((0, 4), (1, 8)))
    inverse_wavelet = jnp.clip(jax.random.uniform(arg_keys[1], (2, F), jnp.float32, -0.05, 0.05), -0.05, 0.05)
    return dict(wavefield=wavefield, inverse_wavelet=inverse_wavelet)


def tables(count_t, count_f, first):
    times = jnp.arange(count_t, dtype=jnp.int32)
    freqs = first + jnp.arange(count_f, dtype=jnp.int32)
    phase = freqs[:, None] * times[None, :] % count_t
    angle = phase.astype(jnp.float32) * (2.0 * math.pi / count_t)
    rows = jnp.stack([jnp.cos(angle), -jnp.sin(angle)], 1).reshape(2 * count_f, count_t)
    forward = (rows / math.sqrt(count_t)).astype(jnp.bfloat16)
    inverse = (rows / math.sqrt(count_f)).astype(jnp.bfloat16)
    return (forward, inverse)

def combine(mirror_real, mirror_imag, sq_real, sq_imag, cube_real, cube_imag, wave_real, wave_imag):
    two_real = wave_real * wave_real - wave_imag * wave_imag
    two_imag = 2.0 * wave_real * wave_imag
    out_real = mirror_real - (wave_real * sq_real - wave_imag * sq_imag) + (two_real * cube_real - two_imag * cube_imag)
    out_imag = mirror_imag - (wave_real * sq_imag + wave_imag * sq_real) + (two_real * cube_imag + two_imag * cube_real)
    return (out_real, out_imag)

def plane_product(left_side, right_side):
    left_side = left_side.astype(jnp.float32)
    right_side = right_side.astype(jnp.float32)
    real_part = jnp.dot(left_side[0], right_side[0]) - jnp.dot(left_side[1], right_side[1])
    imag_part = jnp.dot(left_side[0], right_side[1]) + jnp.dot(left_side[1], right_side[0])
    return (real_part, imag_part)

def reference(wavefield, inverse_wavelet):
    forward, inverse = tables(NT, F, F0)
    step_rows = NS // 16
    blocks = wavefield.reshape(16, step_rows, NS, NT)

    def transform(span_rows):
        return jnp.einsum('ct,srt->csr', forward.astype(jnp.float32), span_rows.astype(jnp.float32))
    spectra = lax.map(transform, blocks)
    spectra = jnp.moveaxis(spectra, 0, 1).reshape(2 * F, NS, NS).astype(jnp.bfloat16).reshape(F, 2, NS, NS)

    def cleaning(inputs):
        spectrum, wavelet = inputs
        values = spectrum.astype(jnp.float32)
        mirrored = (0.5 * (values + jnp.swapaxes(values, 1, 2))).astype(jnp.bfloat16)
        sq_real, sq_imag = plane_product(mirrored, mirrored)
        squared = jnp.stack([sq_real, sq_imag]).astype(jnp.bfloat16)
        cube_real, cube_imag = plane_product(squared, mirrored)
        out_real, out_imag = combine(mirrored[0].astype(jnp.float32), mirrored[1].astype(jnp.float32), sq_real, sq_imag, cube_real, cube_imag, wavelet[0], wavelet[1])
        return jnp.stack([out_real, out_imag]).astype(jnp.bfloat16)
    cleaned = lax.map(cleaning, (spectra, inverse_wavelet.T))
    coeffs = jnp.moveaxis(cleaned.reshape(2 * F, 16, step_rows, NS), 1, 0)

    def back_transform(span_coeffs):
        return jnp.einsum('csr,ct->srt', span_coeffs.astype(jnp.float32), inverse.astype(jnp.float32)).astype(jnp.bfloat16)
    return lax.map(back_transform, coeffs).reshape(NS, NS, NT)
```

```python
import math

import jax
import jax.numpy as jnp
from jax import lax
from jax.sharding import PartitionSpec as P

F0 = 8


def tables(count_t, count_f, first):
    times = jnp.arange(count_t, dtype=jnp.int32)
    freqs = first + jnp.arange(count_f, dtype=jnp.int32)
    phase = freqs[:, None] * times[None, :] % count_t
    angle = phase.astype(jnp.float32) * (2.0 * math.pi / count_t)
    rows = jnp.stack([jnp.cos(angle), -jnp.sin(angle)], 1).reshape(2 * count_f, count_t)
    forward = (rows / math.sqrt(count_t)).astype(jnp.bfloat16)
    inverse = (rows / math.sqrt(count_f)).astype(jnp.bfloat16)
    return (forward, inverse)


def combine(mirror_real, mirror_imag, sq_real, sq_imag, cube_real, cube_imag, wave_real, wave_imag):
    two_real = wave_real * wave_real - wave_imag * wave_imag
    two_imag = 2.0 * wave_real * wave_imag
    out_real = (
        mirror_real
        - (wave_real * sq_real - wave_imag * sq_imag)
        + (two_real * cube_real - two_imag * cube_imag)
    )
    out_imag = (
        mirror_imag
        - (wave_real * sq_imag + wave_imag * sq_real)
        + (two_real * cube_imag + two_imag * cube_real)
    )
    return (out_real, out_imag)


def multiply(left_side, right_side):
    return jnp.einsum("fmk,fkn->fmn", left_side, right_side, preferred_element_type=jnp.float32)


def complex_product(left_side, right_side):
    real_part = multiply(left_side[:, 0], right_side[:, 0]) - multiply(
        left_side[:, 1], right_side[:, 1]
    )
    imag_part = multiply(left_side[:, 0], right_side[:, 1]) + multiply(
        left_side[:, 1], right_side[:, 0]
    )
    return (real_part, imag_part)


def local_sliced(wavefield, inverse_wavelet):
    src_rows, rcv_cols, samples = wavefield.shape
    count_f = inverse_wavelet.shape[1]
    groups = lax.axis_size("rcv")
    per_dev = count_f // groups
    forward, inverse = tables(samples, count_f, F0)
    spectra = jnp.einsum(
        "ct,srt->csr", forward, wavefield, preferred_element_type=jnp.float32
    ).astype(jnp.bfloat16)
    spectra = spectra.reshape(groups, 2 * per_dev, src_rows, rcv_cols)
    slices = lax.all_to_all(spectra, "rcv", split_axis=0, concat_axis=3, tiled=True)
    total_cols = slices.shape[3]
    slices = slices.reshape(per_dev, 2, src_rows, total_cols)
    whole = lax.all_gather(slices, "src", axis=2, tiled=True).astype(jnp.float32)
    all_rows = (0.5 * (whole + jnp.swapaxes(whole, 2, 3))).astype(jnp.bfloat16)
    mirrored = lax.dynamic_slice_in_dim(all_rows, lax.axis_index("src") * src_rows, src_rows, 2)
    sq_real, sq_imag = complex_product(mirrored, all_rows)
    squared = jnp.stack([sq_real, sq_imag], 1).astype(jnp.bfloat16)
    cube_real, cube_imag = complex_product(squared, all_rows)
    wavelet = lax.dynamic_slice_in_dim(inverse_wavelet, lax.axis_index("rcv") * per_dev, per_dev, 1)
    wave_real = wavelet[0][:, None, None]
    wave_imag = wavelet[1][:, None, None]
    out_real, out_imag = combine(
        mirrored[:, 0].astype(jnp.float32),
        mirrored[:, 1].astype(jnp.float32),
        sq_real,
        sq_imag,
        cube_real,
        cube_imag,
        wave_real,
        wave_imag,
    )
    cleaned = (
        jnp.stack([out_real, out_imag], 1)
        .astype(jnp.bfloat16)
        .reshape(1, 2 * per_dev, src_rows, total_cols)
    )
    returned = lax.all_to_all(cleaned, "rcv", split_axis=3, concat_axis=0, tiled=True)
    returned = returned.reshape(2 * count_f, src_rows, rcv_cols)
    return jnp.einsum("csr,ct->srt", returned, inverse, preferred_element_type=jnp.float32).astype(
        jnp.bfloat16
    )


AXES = ("src", "rcv")


def owned_frequency(matrix, wave_real, wave_imag):
    values = matrix.astype(jnp.float32)
    mirrored = (0.5 * (values + jnp.swapaxes(values, 1, 2))).astype(jnp.bfloat16)
    whole = mirrored[None]
    sq_real, sq_imag = complex_product(whole, whole)
    squared = jnp.stack([sq_real, sq_imag], 1).astype(jnp.bfloat16)
    cube_real, cube_imag = complex_product(squared, whole)
    out_real, out_imag = combine(
        mirrored[0].astype(jnp.float32),
        mirrored[1].astype(jnp.float32),
        sq_real[0],
        sq_imag[0],
        cube_real[0],
        cube_imag[0],
        wave_real,
        wave_imag,
    )
    return out_real.astype(jnp.bfloat16), out_imag.astype(jnp.bfloat16)


def local_whole(wavefield, inverse_wavelet):
    src_rows, rcv_cols, samples = wavefield.shape
    count_f = inverse_wavelet.shape[1]
    sources, groups = lax.axis_size("src"), lax.axis_size("rcv")
    devices = sources * groups
    me = lax.axis_index(AXES)
    forward, inverse = tables(samples, count_f, F0)
    chunks = count_f // devices
    width = 2 * devices
    returned = []
    for chunk in range(chunks):
        rows = slice(chunk * width, (chunk + 1) * width)
        spectra = jnp.einsum(
            "ct,srt->csr", forward[rows], wavefield, preferred_element_type=jnp.float32
        ).astype(jnp.bfloat16)
        spectra = spectra.reshape(devices, 2, src_rows, rcv_cols)
        slices = lax.all_to_all(spectra, AXES, 0, 0, tiled=True)
        slices = slices.reshape(sources, groups, 2, src_rows, rcv_cols)
        matrix = slices.transpose(2, 0, 3, 1, 4).reshape(
            2, sources * src_rows, groups * rcv_cols
        )
        wavelet = lax.dynamic_index_in_dim(
            inverse_wavelet, chunk * devices + me, 1, keepdims=False
        )
        out_real, out_imag = owned_frequency(matrix, wavelet[0], wavelet[1])
        cleaned = jnp.stack([out_real, out_imag]).reshape(
            2, sources, src_rows, groups, rcv_cols
        )
        cleaned = cleaned.transpose(1, 3, 0, 2, 4).reshape(devices, 2, src_rows, rcv_cols)
        back = lax.all_to_all(cleaned, AXES, 0, 0, tiled=True)
        returned.append(back.reshape(width, src_rows, rcv_cols))
    total = jnp.concatenate(returned, 0)
    return jnp.einsum("csr,ct->srt", total, inverse, preferred_element_type=jnp.float32).astype(
        jnp.bfloat16
    )


def solution(mesh):
    placed = (P("src", "rcv", None), P())

    def local(wavefield, inverse_wavelet):
        devices = lax.axis_size("src") * lax.axis_size("rcv")
        if inverse_wavelet.shape[1] % devices:
            return local_sliced(wavefield, inverse_wavelet)
        return local_whole(wavefield, inverse_wavelet)

    return jax.shard_map(
        local, mesh=mesh, in_specs=placed, out_specs=P("src", "rcv", None), check_vma=False
    )
```

```python
import functools
import math

import jax
import jax.numpy as jnp
from jax import lax
from jax.experimental import pallas as pl
from jax.experimental.pallas import tpu as pltpu
from jax.sharding import PartitionSpec as P

F0 = 8


def tables(count_t, count_f, first):
    times = jnp.arange(count_t, dtype=jnp.int32)
    freqs = first + jnp.arange(count_f, dtype=jnp.int32)
    phase = freqs[:, None] * times[None, :] % count_t
    angle = phase.astype(jnp.float32) * (2.0 * math.pi / count_t)
    rows = jnp.stack([jnp.cos(angle), -jnp.sin(angle)], 1).reshape(2 * count_f, count_t)
    forward = (rows / math.sqrt(count_t)).astype(jnp.bfloat16)
    inverse = (rows / math.sqrt(count_f)).astype(jnp.bfloat16)
    return (forward, inverse)


def combine(mirror_real, mirror_imag, sq_real, sq_imag, cube_real, cube_imag, wave_real, wave_imag):
    two_real = wave_real * wave_real - wave_imag * wave_imag
    two_imag = 2.0 * wave_real * wave_imag
    out_real = (
        mirror_real
        - (wave_real * sq_real - wave_imag * sq_imag)
        + (two_real * cube_real - two_imag * cube_imag)
    )
    out_imag = (
        mirror_imag
        - (wave_real * sq_imag + wave_imag * sq_real)
        + (two_real * cube_imag + two_imag * cube_real)
    )
    return (out_real, out_imag)


def multiply(left_side, right_side):
    return jnp.einsum("fmk,fkn->fmn", left_side, right_side, preferred_element_type=jnp.float32)


def complex_product(left_side, right_side):
    real_part = multiply(left_side[:, 0], right_side[:, 0]) - multiply(
        left_side[:, 1], right_side[:, 1]
    )
    imag_part = multiply(left_side[:, 0], right_side[:, 1]) + multiply(
        left_side[:, 1], right_side[:, 0]
    )
    return (real_part, imag_part)


def local_sliced(wavefield, inverse_wavelet):
    src_rows, rcv_cols, samples = wavefield.shape
    count_f = inverse_wavelet.shape[1]
    groups = lax.axis_size("rcv")
    per_dev = count_f // groups
    forward, inverse = tables(samples, count_f, F0)
    spectra = jnp.einsum(
        "ct,srt->csr", forward, wavefield, preferred_element_type=jnp.float32
    ).astype(jnp.bfloat16)
    spectra = spectra.reshape(groups, 2 * per_dev, src_rows, rcv_cols)
    slices = lax.all_to_all(spectra, "rcv", split_axis=0, concat_axis=3, tiled=True)
    total_cols = slices.shape[3]
    slices = slices.reshape(per_dev, 2, src_rows, total_cols)
    whole = lax.all_gather(slices, "src", axis=2, tiled=True).astype(jnp.float32)
    all_rows = (0.5 * (whole + jnp.swapaxes(whole, 2, 3))).astype(jnp.bfloat16)
    mirrored = lax.dynamic_slice_in_dim(all_rows, lax.axis_index("src") * src_rows, src_rows, 2)
    sq_real, sq_imag = complex_product(mirrored, all_rows)
    squared = jnp.stack([sq_real, sq_imag], 1).astype(jnp.bfloat16)
    cube_real, cube_imag = complex_product(squared, all_rows)
    wavelet = lax.dynamic_slice_in_dim(inverse_wavelet, lax.axis_index("rcv") * per_dev, per_dev, 1)
    wave_real = wavelet[0][:, None, None]
    wave_imag = wavelet[1][:, None, None]
    out_real, out_imag = combine(
        mirrored[:, 0].astype(jnp.float32),
        mirrored[:, 1].astype(jnp.float32),
        sq_real,
        sq_imag,
        cube_real,
        cube_imag,
        wave_real,
        wave_imag,
    )
    cleaned = (
        jnp.stack([out_real, out_imag], 1)
        .astype(jnp.bfloat16)
        .reshape(1, 2 * per_dev, src_rows, total_cols)
    )
    returned = lax.all_to_all(cleaned, "rcv", split_axis=3, concat_axis=0, tiled=True)
    returned = returned.reshape(2 * count_f, src_rows, rcv_cols)
    return jnp.einsum("csr,ct->srt", returned, inverse, preferred_element_type=jnp.float32).astype(
        jnp.bfloat16
    )


NT_DIMS = (((1,), (1,)), ((), ()))
TN_DIMS = (((0,), (0,)), ((), ()))

def dft_kernel(table_ref, wave_ref, out_ref, held):
    rows, cols, samples = wave_ref.shape
    bins = table_ref.shape[0]
    flat = wave_ref[...].reshape(rows * cols, samples)
    spec = lax.dot_general(table_ref[...], flat, NT_DIMS, preferred_element_type=jnp.float32)
    for row in range(rows):
        held[pl.ds(row, bins, stride=rows), :] = spec[:, row * cols:(row + 1) * cols]
    out_ref[...] = held[...].reshape(bins, rows, cols).astype(out_ref.dtype)

def dft(table, wave, step=16):
    rows, cols, samples = wave.shape
    bins = table.shape[0]
    return pl.pallas_call(
        dft_kernel, grid=(rows // step,),
        in_specs=[pl.BlockSpec((bins, samples), lambda i: (0, 0)),
                  pl.BlockSpec((step, cols, samples), lambda i: (i, 0, 0))],
        out_specs=pl.BlockSpec((bins, step, cols), lambda i: (0, i, 0)),
        out_shape=jax.ShapeDtypeStruct((bins, rows, cols), jnp.bfloat16),
        scratch_shapes=[pltpu.VMEM((bins * step, cols), jnp.float32)],
        cost_estimate=pl.CostEstimate(flops=2 * bins * samples * rows * cols, bytes_accessed=2 * rows * cols * (samples + bins), transcendentals=0),
        name="forward_table",
    )(table, wave)

def inverse_kernel(table_ref, *refs):
    *coeffs, out_ref, held = refs
    rows, cols, samples = out_ref.shape
    start = 0
    for ref in coeffs:
        n = ref.shape[0]
        held[start * rows:(start + n) * rows, :] = ref[...].astype(jnp.float32).reshape(n * rows, cols)
        start += n
    table = table_ref[...]
    for row in range(rows):
        lhs = held[pl.ds(row, start, stride=rows), :].astype(jnp.bfloat16)
        out_ref[row] = lax.dot_general(lhs, table, TN_DIMS, preferred_element_type=jnp.float32).astype(out_ref.dtype)

def inverse_t(table, coeffs, step=16):
    bins, samples = table.shape
    _, rows, cols = coeffs[0].shape
    return pl.pallas_call(
        inverse_kernel, grid=(rows // step,),
        in_specs=[pl.BlockSpec((bins, samples), lambda i: (0, 0))] +
                 [pl.BlockSpec((c.shape[0], step, cols), lambda i: (0, i, 0)) for c in coeffs],
        out_specs=pl.BlockSpec((step, cols, samples), lambda i: (i, 0, 0)),
        out_shape=jax.ShapeDtypeStruct((rows, cols, samples), jnp.bfloat16),
        scratch_shapes=[pltpu.VMEM((bins * step, cols), jnp.float32)],
        cost_estimate=pl.CostEstimate(flops=2 * bins * samples * rows * cols, bytes_accessed=2 * rows * cols * (samples + bins), transcendentals=0),
        name="inverse_table",
    )(table, *coeffs)

def owner_kernel(wave_ref, recv_ref, out_ref, held, *, sources, groups):
    _, _, rows, cols = recv_ref.shape
    per = rows // cols
    total = sources * rows
    def mirror(block, carry):
        src, half = block // per, block % per
        for part in range(2):
            for col in range(groups):
                a = recv_ref[src * groups + col, part, pl.ds(pl.multiple_of(half * cols, cols), cols), :].astype(jnp.float32)
                b = recv_ref[(col // per) * groups + block, part, (col % per) * cols:(col % per + 1) * cols, :].astype(jnp.float32)
                held[part, pl.ds(pl.multiple_of(block * cols, cols), cols), col * cols:(col + 1) * cols] = (0.5 * (a + b.T)).astype(jnp.bfloat16)
        return carry
    lax.fori_loop(0, groups, mirror, 0)
    wr, wi = wave_ref[0], wave_ref[1]
    tr, ti = wr * wr - wi * wi, 2.0 * wr * wi
    def dot(a, b): return jnp.dot(a, b, preferred_element_type=jnp.float32)
    def product(src, carry):
        sl = pl.ds(pl.multiple_of(src * rows, rows), rows)
        mr, mi = held[0, sl, :], held[1, sl, :]
        sr = dot(mr, held[0]) - dot(mi, held[1])
        si = dot(mr, held[1]) + dot(mi, held[0])
        br, bi = sr.astype(jnp.bfloat16), si.astype(jnp.bfloat16)
        cr = dot(br, held[0]) - dot(bi, held[1])
        ore = mr.astype(jnp.float32) - (wr * sr - wi * si) + (tr * cr)
        oim = mi.astype(jnp.float32) - (wr * si + wi * sr) + (ti * cr)
        ci = dot(br, held[1]) + dot(bi, held[0])
        ore = (ore - ti * ci).astype(out_ref.dtype)
        oim = (oim + tr * ci).astype(out_ref.dtype)
        for col in range(groups):
            out_ref[src * groups + col, 0] = ore[:, col * cols:(col + 1) * cols]
            out_ref[src * groups + col, 1] = oim[:, col * cols:(col + 1) * cols]
        return carry
    lax.fori_loop(0, sources, product, 0)

def owner(wave, recv, sources, groups):
    devices, _, rows, cols = recv.shape
    total = sources * rows
    return pl.pallas_call(
        functools.partial(owner_kernel, sources=sources, groups=groups),
        in_specs=[pl.BlockSpec(memory_space=pltpu.SMEM), pl.BlockSpec(memory_space=pltpu.VMEM)],
        out_specs=pl.BlockSpec(memory_space=pltpu.VMEM),
        out_shape=jax.ShapeDtypeStruct(recv.shape, recv.dtype),
        scratch_shapes=[pltpu.VMEM((2, total, total), jnp.bfloat16)],
        cost_estimate=pl.CostEstimate(flops=16 * total**3, bytes_accessed=4 * recv.size, transcendentals=0),
        compiler_params=pltpu.CompilerParams(vmem_limit_bytes=56 << 20),
        name="owned_frequency",
    )(wave, recv)


AXES = ("src", "rcv")


def local_whole(wavefield, inverse_wavelet):
    src_rows, rcv_cols, samples = wavefield.shape
    count_f = inverse_wavelet.shape[1]
    sources, groups = lax.axis_size("src"), lax.axis_size("rcv")
    devices = sources * groups
    me = lax.axis_index(AXES)
    forward, inverse = tables(samples, count_f, F0)
    width = 2 * devices
    returned = []
    for chunk in range(count_f // devices):
        spectra = dft(forward[chunk * width : (chunk + 1) * width], wavefield, 64)
        spectra = spectra.reshape(devices, 2, src_rows, rcv_cols)
        slices = lax.all_to_all(spectra, AXES, 0, 0, tiled=True)
        wavelet = lax.dynamic_index_in_dim(
            inverse_wavelet, chunk * devices + me, 1, keepdims=False
        )
        cleaned = owner(wavelet, slices, sources, groups)
        back = lax.all_to_all(cleaned, AXES, 0, 0, tiled=True)
        returned.append(back.reshape(width, src_rows, rcv_cols))
    return inverse_t(inverse, returned, 16)


def solution(mesh):
    placed = (P("src", "rcv", None), P())

    def local(wavefield, inverse_wavelet):
        devices = lax.axis_size("src") * lax.axis_size("rcv")
        if inverse_wavelet.shape[1] % devices:
            return local_sliced(wavefield, inverse_wavelet)
        return local_whole(wavefield, inverse_wavelet)

    return jax.shard_map(
        local, mesh=mesh, in_specs=placed, out_specs=P("src", "rcv", None), check_vma=False
    )
```

```python
import functools
import math

import jax
import jax.numpy as jnp
from jax import lax
from jax.experimental import pallas as pl
from jax.experimental.pallas import tpu as pltpu
from jax.sharding import PartitionSpec as P

F0 = 8


def tables(count_t, count_f, first):
    times = jnp.arange(count_t, dtype=jnp.int32)
    freqs = first + jnp.arange(count_f, dtype=jnp.int32)
    phase = freqs[:, None] * times[None, :] % count_t
    angle = phase.astype(jnp.float32) * (2.0 * math.pi / count_t)
    rows = jnp.stack([jnp.cos(angle), -jnp.sin(angle)], 1).reshape(2 * count_f, count_t)
    forward = (rows / math.sqrt(count_t)).astype(jnp.bfloat16)
    inverse = (rows / math.sqrt(count_f)).astype(jnp.bfloat16)
    return (forward, inverse)


def combine(mirror_real, mirror_imag, sq_real, sq_imag, cube_real, cube_imag, wave_real, wave_imag):
    two_real = wave_real * wave_real - wave_imag * wave_imag
    two_imag = 2.0 * wave_real * wave_imag
    out_real = (
        mirror_real
        - (wave_real * sq_real - wave_imag * sq_imag)
        + (two_real * cube_real - two_imag * cube_imag)
    )
    out_imag = (
        mirror_imag
        - (wave_real * sq_imag + wave_imag * sq_real)
        + (two_real * cube_imag + two_imag * cube_real)
    )
    return (out_real, out_imag)


def multiply(left_side, right_side):
    return jnp.einsum("fmk,fkn->fmn", left_side, right_side, preferred_element_type=jnp.float32)


def complex_product(left_side, right_side):
    real_part = multiply(left_side[:, 0], right_side[:, 0]) - multiply(
        left_side[:, 1], right_side[:, 1]
    )
    imag_part = multiply(left_side[:, 0], right_side[:, 1]) + multiply(
        left_side[:, 1], right_side[:, 0]
    )
    return (real_part, imag_part)


def local_sliced(wavefield, inverse_wavelet):
    src_rows, rcv_cols, samples = wavefield.shape
    count_f = inverse_wavelet.shape[1]
    groups = lax.axis_size("rcv")
    per_dev = count_f // groups
    forward, inverse = tables(samples, count_f, F0)
    spectra = jnp.einsum(
        "ct,srt->csr", forward, wavefield, preferred_element_type=jnp.float32
    ).astype(jnp.bfloat16)
    spectra = spectra.reshape(groups, 2 * per_dev, src_rows, rcv_cols)
    slices = lax.all_to_all(spectra, "rcv", split_axis=0, concat_axis=3, tiled=True)
    total_cols = slices.shape[3]
    slices = slices.reshape(per_dev, 2, src_rows, total_cols)
    whole = lax.all_gather(slices, "src", axis=2, tiled=True).astype(jnp.float32)
    all_rows = (0.5 * (whole + jnp.swapaxes(whole, 2, 3))).astype(jnp.bfloat16)
    mirrored = lax.dynamic_slice_in_dim(all_rows, lax.axis_index("src") * src_rows, src_rows, 2)
    sq_real, sq_imag = complex_product(mirrored, all_rows)
    squared = jnp.stack([sq_real, sq_imag], 1).astype(jnp.bfloat16)
    cube_real, cube_imag = complex_product(squared, all_rows)
    wavelet = lax.dynamic_slice_in_dim(inverse_wavelet, lax.axis_index("rcv") * per_dev, per_dev, 1)
    wave_real = wavelet[0][:, None, None]
    wave_imag = wavelet[1][:, None, None]
    out_real, out_imag = combine(
        mirrored[:, 0].astype(jnp.float32),
        mirrored[:, 1].astype(jnp.float32),
        sq_real,
        sq_imag,
        cube_real,
        cube_imag,
        wave_real,
        wave_imag,
    )
    cleaned = (
        jnp.stack([out_real, out_imag], 1)
        .astype(jnp.bfloat16)
        .reshape(1, 2 * per_dev, src_rows, total_cols)
    )
    returned = lax.all_to_all(cleaned, "rcv", split_axis=3, concat_axis=0, tiled=True)
    returned = returned.reshape(2 * count_f, src_rows, rcv_cols)
    return jnp.einsum("csr,ct->srt", returned, inverse, preferred_element_type=jnp.float32).astype(
        jnp.bfloat16
    )


NT_DIMS = (((1,), (1,)), ((), ()))
TN_DIMS = (((0,), (0,)), ((), ()))

def dft_kernel(table_ref, wave_ref, out_ref, held):
    rows, cols, samples = wave_ref.shape
    bins = table_ref.shape[0]
    flat = wave_ref[...].reshape(rows * cols, samples)
    spec = lax.dot_general(table_ref[...], flat, NT_DIMS, preferred_element_type=jnp.float32)
    for row in range(rows):
        held[pl.ds(row, bins, stride=rows), :] = spec[:, row * cols:(row + 1) * cols]
    out_ref[...] = held[...].reshape(bins, rows, cols).astype(out_ref.dtype)

def dft(table, wave, step=16):
    rows, cols, samples = wave.shape
    bins = table.shape[0]
    return pl.pallas_call(
        dft_kernel, grid=(rows // step,),
        in_specs=[pl.BlockSpec((bins, samples), lambda i: (0, 0)),
                  pl.BlockSpec((step, cols, samples), lambda i: (i, 0, 0))],
        out_specs=pl.BlockSpec((bins, step, cols), lambda i: (0, i, 0)),
        out_shape=jax.ShapeDtypeStruct((bins, rows, cols), jnp.bfloat16),
        scratch_shapes=[pltpu.VMEM((bins * step, cols), jnp.float32)],
        cost_estimate=pl.CostEstimate(flops=2 * bins * samples * rows * cols, bytes_accessed=2 * rows * cols * (samples + bins), transcendentals=0),
        name="forward_table",
    )(table, wave)

def inverse_kernel(table_ref, *refs):
    *coeffs, out_ref, held = refs
    rows, cols, samples = out_ref.shape
    start = 0
    for ref in coeffs:
        n = ref.shape[0]
        held[start * rows:(start + n) * rows, :] = ref[...].astype(jnp.float32).reshape(n * rows, cols)
        start += n
    table = table_ref[...]
    for row in range(rows):
        lhs = held[pl.ds(row, start, stride=rows), :].astype(jnp.bfloat16)
        out_ref[row] = lax.dot_general(lhs, table, TN_DIMS, preferred_element_type=jnp.float32).astype(out_ref.dtype)

def inverse_t(table, coeffs, step=16):
    bins, samples = table.shape
    _, rows, cols = coeffs[0].shape
    return pl.pallas_call(
        inverse_kernel, grid=(rows // step,),
        in_specs=[pl.BlockSpec((bins, samples), lambda i: (0, 0))] +
                 [pl.BlockSpec((c.shape[0], step, cols), lambda i: (0, i, 0)) for c in coeffs],
        out_specs=pl.BlockSpec((step, cols, samples), lambda i: (i, 0, 0)),
        out_shape=jax.ShapeDtypeStruct((rows, cols, samples), jnp.bfloat16),
        scratch_shapes=[pltpu.VMEM((bins * step, cols), jnp.float32)],
        cost_estimate=pl.CostEstimate(flops=2 * bins * samples * rows * cols, bytes_accessed=2 * rows * cols * (samples + bins), transcendentals=0),
        name="inverse_table",
    )(table, *coeffs)


def tri(value, other, upper):
    row = lax.broadcasted_iota(jnp.int32, value.shape, 0)
    col = lax.broadcasted_iota(jnp.int32, value.shape, 1)
    return jnp.where(row <= col, value, other) if upper else jnp.where(row > col, value, other)


def diagonal(value):
    row = lax.broadcasted_iota(jnp.int32, value.shape, 0)
    col = lax.broadcasted_iota(jnp.int32, value.shape, 1)
    return jnp.sum(jnp.where(row == col, value, 0.0), axis=0, keepdims=True)


def with_diagonal(value, line):
    row = lax.broadcasted_iota(jnp.int32, value.shape, 0)
    col = lax.broadcasted_iota(jnp.int32, value.shape, 1)
    return jnp.where(row == col, jnp.broadcast_to(line, value.shape), value)


EXTRA = 8


def fold_kernel(place_ref, whole_ref, swap_ref, *refs):
    *hand_refs, out_ref = refs
    count, length, cols = whole_ref.shape
    piece = hand_refs[0].shape[1]
    kept = length - piece
    diagonal_device, side = place_ref[0], place_ref[1]

    def each(d, carry):
        @pl.when(diagonal_device == 1)
        def _():
            for half in range(2):
                real = whole_ref[d, half * cols : (half + 1) * cols].astype(jnp.float32)
                imag = whole_ref[d, (2 + half) * cols : (3 + half) * cols].astype(jnp.float32)
                span = slice(half * cols, (half + 1) * cols)

                @pl.when(side == half)
                def _():
                    mean_real = 0.5 * (real + real.T)
                    mean_imag = 0.5 * (imag + imag.T)
                    out_ref[d, span] = tri(mean_real, mean_imag, True).astype(out_ref.dtype)
                    line = jnp.broadcast_to(diagonal(mean_imag), (EXTRA, cols))
                    out_ref[d, kept:] = line.astype(out_ref.dtype)

                @pl.when(side != half)
                def _():
                    own = imag if half else real
                    mean = 0.5 * (own + swap_ref[d].astype(jnp.float32).T)
                    out_ref[d, span] = mean.astype(out_ref.dtype)

            for index, hand_ref in enumerate(hand_refs):
                start = 2 * cols + index * piece
                out_ref[d, start : start + piece] = hand_ref[d]

        @pl.when(diagonal_device == 0)
        def _():
            out_ref[d, :kept] = whole_ref[d, :kept]
            out_ref[d, kept:] = jnp.zeros((EXTRA, cols), out_ref.dtype)

        return carry

    lax.fori_loop(0, count, each, 0)


def unfold_kernel(place_ref, folded_ref, swap_ref, *refs):
    *hand_refs, out_ref = refs
    count, length, cols = out_ref.shape
    piece = hand_refs[0].shape[1]
    kept = length - piece
    diagonal_device, side, turn = place_ref[0], place_ref[1], place_ref[2]

    def each(d, carry):
        @pl.when(diagonal_device == 1)
        def _():
            for half in range(2):
                own = folded_ref[d, half * cols : (half + 1) * cols]
                real = slice(half * cols, (half + 1) * cols)
                imag = slice((2 + half) * cols, (3 + half) * cols)

                @pl.when(side == half)
                def _():
                    packed = own.astype(jnp.float32)
                    line = folded_ref[d, kept:].astype(jnp.float32)[:1]
                    out_ref[d, real] = tri(packed, packed.T, True).astype(out_ref.dtype)
                    lower = with_diagonal(tri(packed, packed.T, False), line)
                    out_ref[d, imag] = lower.astype(out_ref.dtype)

                @pl.when(side != half)
                def _():
                    other = swap_ref[d].astype(jnp.float32).T.astype(out_ref.dtype)
                    out_ref[d, imag if half else real] = own
                    out_ref[d, real if half else imag] = other

        @pl.when(diagonal_device == 0)
        def _():
            out_ref[d, :kept] = folded_ref[d, :kept]

            for index, hand_ref in enumerate(hand_refs):

                @pl.when(turn == index + 1)
                def _():
                    out_ref[d, kept:] = hand_ref[d]

        return carry

    lax.fori_loop(0, count, each, 0)


def per_device(kernel, place, first, swap, hands, shape, name, step=4):
    devices = first.shape[0]

    def spec(array_shape):
        rest = len(array_shape) - 1
        return pl.BlockSpec((step,) + tuple(array_shape[1:]), lambda i: (i,) + (0,) * rest)

    return pl.pallas_call(
        kernel,
        grid=(devices // step,),
        in_specs=[pl.BlockSpec(memory_space=pltpu.SMEM)]
        + [spec(a.shape) for a in (first, swap, *hands)],
        out_specs=spec(shape),
        out_shape=jax.ShapeDtypeStruct(shape, first.dtype),
        cost_estimate=pl.CostEstimate(
            flops=4 * first.size, bytes_accessed=8 * first.size, transcendentals=0
        ),
        name=name,
    )(place, first, swap, *hands)


def owner_kernel(wave_ref, recv_ref, out_ref, held, done, *, sources, groups, cols, fold_in, fold_out):
    halves = groups // sources
    rows = halves * cols
    piece = cols // 2
    kept = 2 * rows - piece

    def at(block):
        return pl.ds(pl.multiple_of(block * cols, cols), cols)

    def load(d, start):
        return recv_ref[d, start * cols : (start + 1) * cols].astype(jnp.float32)

    def slot(turn):
        return slice(2 * cols + (turn - 1) * piece, 2 * cols + turn * piece)

    def load_kept(part, half, src, col, owner_src, turn):
        if part == 0 or half == 0:
            return load(src * groups + col, part * halves + half)
        upper = recv_ref[src * groups + col, kept - piece : kept].astype(jnp.float32)
        lower = recv_ref[owner_src * groups + col, slot(turn)].astype(jnp.float32)
        return jnp.concatenate([upper, lower], 0)

    def put(part, row, col, value):
        held[part, at(row), at(col)] = value.astype(jnp.bfloat16)

    def mirror_whole(src, carry):
        for half in range(halves):
            block = src * halves + half
            for part in range(2):
                for col in range(groups):
                    a = load(src * groups + col, part * halves + half)
                    b = load((col // halves) * groups + block, part * halves + col % halves)
                    put(part, block, col, 0.5 * (a + b.T))
        return carry

    def mirror_folded(src, carry):
        for turn in range(1, sources):
            other = src ^ turn
            for half in range(halves):
                row = src * halves + half
                for side in range(halves):
                    col = other * halves + side
                    for part in range(2):
                        a = load_kept(part, half, src, col, other, turn)
                        b = load_kept(part, side, other, row, src, turn)
                        put(part, row, col, 0.5 * (a + b.T))
        low, high = src * halves, src * halves + 1
        for side in range(halves):
            block = src * halves + side
            d = src * groups + block
            packed = load(d, side)
            line = recv_ref[d, kept:].astype(jnp.float32)[:1]
            put(0, block, block, tri(packed, packed.T, True))
            put(1, block, block, with_diagonal(tri(packed, packed.T, False), line))
        real = load(src * groups + high, 0)
        imag = load(src * groups + low, 1)
        put(0, low, high, real)
        put(0, high, low, real.T)
        put(1, high, low, imag)
        put(1, low, high, imag.T)
        return carry

    lax.fori_loop(0, sources, mirror_folded if fold_in else mirror_whole, 0)

    wave_real, wave_imag = wave_ref[0], wave_ref[1]
    two_real = wave_real * wave_real - wave_imag * wave_imag
    two_imag = 2.0 * wave_real * wave_imag

    def dot(left, right):
        return jnp.dot(left, right, preferred_element_type=jnp.float32)

    def product(src, carry):
        span = pl.ds(pl.multiple_of(src * rows, rows), rows)
        real, imag = held[0, span, :], held[1, span, :]
        sq_real = dot(real, held[0]) - dot(imag, held[1])
        sq_imag = dot(real, held[1]) + dot(imag, held[0])
        out_real = real.astype(jnp.float32) - (wave_real * sq_real - wave_imag * sq_imag)
        out_imag = imag.astype(jnp.float32) - (wave_real * sq_imag + wave_imag * sq_real)
        left_real, left_imag = sq_real.astype(jnp.bfloat16), sq_imag.astype(jnp.bfloat16)
        cube_real = dot(left_real, held[0]) - dot(left_imag, held[1])
        cube_imag = dot(left_real, held[1]) + dot(left_imag, held[0])
        out_real = (out_real + (two_real * cube_real - two_imag * cube_imag)).astype(jnp.bfloat16)
        out_imag = (out_imag + (two_real * cube_imag + two_imag * cube_real)).astype(jnp.bfloat16)
        if fold_out:
            done[0, span, :] = out_real
            done[1, span, :] = out_imag
        else:
            for col in range(groups):
                out_ref[src * groups + col, :rows] = out_real[:, col * cols : (col + 1) * cols]
                out_ref[src * groups + col, rows:] = out_imag[:, col * cols : (col + 1) * cols]
        return carry

    lax.fori_loop(0, sources, product, 0)
    if not fold_out:
        return

    def pack(src, carry):
        span = pl.ds(pl.multiple_of(src * rows, rows), rows)
        for turn in range(1, sources):
            other = src ^ turn
            for side in range(halves):
                col = other * halves + side
                d = src * groups + col
                imag = done[1, span, at(col)]
                out_ref[d, :rows] = done[0, span, at(col)]
                out_ref[d, rows:kept] = imag[: rows - piece]
                out_ref[d, kept:] = jnp.zeros((EXTRA, cols), jnp.bfloat16)
                out_ref[other * groups + col, slot(turn)] = imag[rows - piece :]
        for side in range(halves):
            block = src * halves + side
            d = src * groups + block
            real = done[0, at(block), at(block)].astype(jnp.float32)
            imag = done[1, at(block), at(block)].astype(jnp.float32)
            out_ref[d, side * cols : (side + 1) * cols] = tri(real, imag, True).astype(jnp.bfloat16)
            line = jnp.broadcast_to(diagonal(imag), (EXTRA, cols))
            out_ref[d, kept:] = line.astype(jnp.bfloat16)
        low, high = src * halves, src * halves + 1
        out_ref[src * groups + high, :cols] = done[0, at(low), at(high)]
        out_ref[src * groups + low, cols : 2 * cols] = done[1, at(high), at(low)]
        return carry

    lax.fori_loop(0, sources, pack, 0)


def owner(wave, recv, sources, groups, fold_in, fold_out):
    devices, length, cols = recv.shape
    total = groups * cols
    whole = 2 * (total // sources)
    out_shape = (devices, whole - cols // 2 + EXTRA if fold_out else whole, cols)
    return pl.pallas_call(
        functools.partial(
            owner_kernel,
            sources=sources,
            groups=groups,
            cols=cols,
            fold_in=fold_in,
            fold_out=fold_out,
        ),
        in_specs=[
            pl.BlockSpec(memory_space=pltpu.SMEM),
            pl.BlockSpec(memory_space=pltpu.VMEM),
        ],
        out_specs=pl.BlockSpec(memory_space=pltpu.VMEM),
        out_shape=jax.ShapeDtypeStruct(out_shape, recv.dtype),
        scratch_shapes=[
            pltpu.VMEM((2, total, total), jnp.bfloat16),
            pltpu.VMEM((2, total, total) if fold_out else (2, 16, 128), jnp.bfloat16),
        ],
        cost_estimate=pl.CostEstimate(
            flops=16 * total**3, bytes_accessed=4 * recv.size, transcendentals=0
        ),
        compiler_params=pltpu.CompilerParams(vmem_limit_bytes=56 << 20),
        name="owned_frequency",
    )(wave, recv)


AXES = ("src", "rcv")


def swap_pairs(sources, groups):
    halves = groups // sources
    return [
        (src * groups + src * halves + side, src * groups + src * halves + 1 - side)
        for src in range(sources)
        for side in range(halves)
    ]


def hand_pairs(sources, groups, turn, back):
    pairs = []
    for col in range(groups):
        src = col // (groups // sources)
        pair = ((src ^ turn) * groups + col, src * groups + col)
        pairs.append(pair[::-1] if back else pair)
    return pairs


def where_am_i(sources, groups):
    halves = groups // sources
    src, col = lax.axis_index("src"), lax.axis_index("rcv")
    turn = src ^ (col // halves)
    return turn, col % halves


def fold(spectra, sources, groups):
    devices, length, cols = spectra.shape
    piece = cols // 2
    turn, side = where_am_i(sources, groups)
    block = lax.dynamic_slice_in_dim(spectra, jnp.where(side == 0, 1, 2) * cols, cols, 1)
    swap = lax.ppermute(block, AXES, swap_pairs(sources, groups))
    last = spectra[:, length - piece :]
    hands = [
        lax.ppermute(last, AXES, hand_pairs(sources, groups, t, False)) for t in range(1, sources)
    ]
    place = jnp.stack([(turn == 0).astype(jnp.int32), side, turn]).astype(jnp.int32)
    shape = (devices, length - piece + EXTRA, cols)
    return per_device(fold_kernel, place, spectra, swap, hands, shape, "fold")


def unfold(folded, sources, groups):
    devices, length, cols = folded.shape
    piece = cols // 2
    turn, side = where_am_i(sources, groups)
    block = lax.dynamic_slice_in_dim(folded, (1 - side) * cols, cols, 1)
    swap = lax.ppermute(block, AXES, swap_pairs(sources, groups))
    hands = []
    for t in range(1, sources):
        start = 2 * cols + (t - 1) * piece
        pairs = hand_pairs(sources, groups, t, True)
        hands.append(lax.ppermute(folded[:, start : start + piece], AXES, pairs))
    place = jnp.stack([(turn == 0).astype(jnp.int32), side, turn]).astype(jnp.int32)
    shape = (devices, length - EXTRA + piece, cols)
    return per_device(unfold_kernel, place, folded, swap, hands, shape, "unfold")


def local_whole(wavefield, inverse_wavelet):
    src_rows, rcv_cols, samples = wavefield.shape
    count_f = inverse_wavelet.shape[1]
    sources, groups = lax.axis_size("src"), lax.axis_size("rcv")
    devices = sources * groups
    me = lax.axis_index(AXES)
    forward, inverse = tables(samples, count_f, F0)
    width = 2 * devices
    chunks = count_f // devices
    returned = []
    for chunk in range(chunks):
        fold_in, fold_out = chunk > 0, chunk < chunks - 1
        spectra = dft(forward[chunk * width : (chunk + 1) * width], wavefield, 64)
        spectra = spectra.reshape(devices, 2 * src_rows, rcv_cols)
        if fold_in:
            spectra = fold(spectra, sources, groups)
        slices = lax.all_to_all(spectra, AXES, 0, 0, tiled=True)
        wavelet = lax.dynamic_index_in_dim(
            inverse_wavelet, chunk * devices + me, 1, keepdims=False
        )
        cleaned = owner(wavelet, slices, sources, groups, fold_in, fold_out)
        back = lax.all_to_all(cleaned, AXES, 0, 0, tiled=True)
        if fold_out:
            back = unfold(back, sources, groups)
        returned.append(back.reshape(width, src_rows, rcv_cols))
    return inverse_t(inverse, returned, 16)


def solution(mesh):
    placed = (P("src", "rcv", None), P())

    def local(wavefield, inverse_wavelet):
        sources, groups = lax.axis_size("src"), lax.axis_size("rcv")
        fits = inverse_wavelet.shape[1] % (sources * groups) == 0
        if fits and sources == 4 and groups == 2 * sources:
            return local_whole(wavefield, inverse_wavelet)
        return local_sliced(wavefield, inverse_wavelet)

    return jax.shard_map(
        local, mesh=mesh, in_specs=placed, out_specs=P("src", "rcv", None), check_vma=False
    )
```

```python
import functools
import math

import jax
import jax.numpy as jnp
from jax import lax
from jax.experimental import pallas as pl
from jax.experimental.pallas import tpu as pltpu
from jax.sharding import PartitionSpec as P

F0 = 8


def tables(count_t, count_f, first):
    times = jnp.arange(count_t, dtype=jnp.int32)
    freqs = first + jnp.arange(count_f, dtype=jnp.int32)
    phase = freqs[:, None] * times[None, :] % count_t
    angle = phase.astype(jnp.float32) * (2.0 * math.pi / count_t)
    rows = jnp.stack([jnp.cos(angle), -jnp.sin(angle)], 1).reshape(2 * count_f, count_t)
    forward = (rows / math.sqrt(count_t)).astype(jnp.bfloat16)
    inverse = (rows / math.sqrt(count_f)).astype(jnp.bfloat16)
    return (forward, inverse)


def combine(mirror_real, mirror_imag, sq_real, sq_imag, cube_real, cube_imag, wave_real, wave_imag):
    two_real = wave_real * wave_real - wave_imag * wave_imag
    two_imag = 2.0 * wave_real * wave_imag
    out_real = (
        mirror_real
        - (wave_real * sq_real - wave_imag * sq_imag)
        + (two_real * cube_real - two_imag * cube_imag)
    )
    out_imag = (
        mirror_imag
        - (wave_real * sq_imag + wave_imag * sq_real)
        + (two_real * cube_imag + two_imag * cube_real)
    )
    return (out_real, out_imag)


def multiply(left_side, right_side):
    return jnp.einsum("fmk,fkn->fmn", left_side, right_side, preferred_element_type=jnp.float32)


def complex_product(left_side, right_side):
    real_part = multiply(left_side[:, 0], right_side[:, 0]) - multiply(
        left_side[:, 1], right_side[:, 1]
    )
    imag_part = multiply(left_side[:, 0], right_side[:, 1]) + multiply(
        left_side[:, 1], right_side[:, 0]
    )
    return (real_part, imag_part)


def local_sliced(wavefield, inverse_wavelet):
    src_rows, rcv_cols, samples = wavefield.shape
    count_f = inverse_wavelet.shape[1]
    groups = lax.axis_size("rcv")
    per_dev = count_f // groups
    forward, inverse = tables(samples, count_f, F0)
    spectra = jnp.einsum(
        "ct,srt->csr", forward, wavefield, preferred_element_type=jnp.float32
    ).astype(jnp.bfloat16)
    spectra = spectra.reshape(groups, 2 * per_dev, src_rows, rcv_cols)
    slices = lax.all_to_all(spectra, "rcv", split_axis=0, concat_axis=3, tiled=True)
    total_cols = slices.shape[3]
    slices = slices.reshape(per_dev, 2, src_rows, total_cols)
    whole = lax.all_gather(slices, "src", axis=2, tiled=True).astype(jnp.float32)
    all_rows = (0.5 * (whole + jnp.swapaxes(whole, 2, 3))).astype(jnp.bfloat16)
    mirrored = lax.dynamic_slice_in_dim(all_rows, lax.axis_index("src") * src_rows, src_rows, 2)
    sq_real, sq_imag = complex_product(mirrored, all_rows)
    squared = jnp.stack([sq_real, sq_imag], 1).astype(jnp.bfloat16)
    cube_real, cube_imag = complex_product(squared, all_rows)
    wavelet = lax.dynamic_slice_in_dim(inverse_wavelet, lax.axis_index("rcv") * per_dev, per_dev, 1)
    wave_real = wavelet[0][:, None, None]
    wave_imag = wavelet[1][:, None, None]
    out_real, out_imag = combine(
        mirrored[:, 0].astype(jnp.float32),
        mirrored[:, 1].astype(jnp.float32),
        sq_real,
        sq_imag,
        cube_real,
        cube_imag,
        wave_real,
        wave_imag,
    )
    cleaned = (
        jnp.stack([out_real, out_imag], 1)
        .astype(jnp.bfloat16)
        .reshape(1, 2 * per_dev, src_rows, total_cols)
    )
    returned = lax.all_to_all(cleaned, "rcv", split_axis=3, concat_axis=0, tiled=True)
    returned = returned.reshape(2 * count_f, src_rows, rcv_cols)
    return jnp.einsum("csr,ct->srt", returned, inverse, preferred_element_type=jnp.float32).astype(
        jnp.bfloat16
    )


NT_DIMS = (((1,), (1,)), ((), ()))
TN_DIMS = (((0,), (0,)), ((), ()))
EDGE = 32


def dft_kernel(table_ref, wave_ref, out_ref, *, group):
    rows, cols, samples = wave_ref.shape
    for first in range(0, rows, group):
        flat = wave_ref[first : first + group].reshape(group * cols, samples)
        values = lax.dot_general(flat, table_ref[...], NT_DIMS, preferred_element_type=jnp.float32)
        turned = [values[row * cols : (row + 1) * cols].T for row in range(group)]
        stacked = jnp.swapaxes(jnp.stack(turned, 0), 0, 1)
        out_ref[:, first : first + group, :] = stacked.astype(out_ref.dtype)


def dft(table, wave, start, count, step):
    _, cols, samples = wave.shape
    bins = table.shape[0]
    skip = start // step
    return pl.pallas_call(
        functools.partial(dft_kernel, group=16),
        grid=(count // step,),
        in_specs=[
            pl.BlockSpec((bins, samples), lambda i: (0, 0)),
            pl.BlockSpec((step, cols, samples), lambda i: (i + skip, 0, 0)),
        ],
        out_specs=pl.BlockSpec((bins, step, cols), lambda i: (0, i, 0)),
        out_shape=jax.ShapeDtypeStruct((bins, count, cols), jnp.bfloat16),
        cost_estimate=pl.CostEstimate(
            flops=2 * bins * samples * count * cols,
            bytes_accessed=2 * count * cols * (samples + bins),
            transcendentals=0,
        ),
        name="forward_table",
    )(table, wave)


def inverse_kernel(table_ref, first_ref, last_ref, *refs):
    out_ref = refs[-1]
    table = table_ref[...]
    both = jnp.swapaxes(jnp.concatenate([first_ref[...], last_ref[...]], 0), 0, 1)
    for row in range(out_ref.shape[0]):
        out_ref[row] = lax.dot_general(
            both[row], table, TN_DIMS, preferred_element_type=jnp.float32
        ).astype(out_ref.dtype)


def inverse_rows(table, first, last, start, step, prior=None):
    bins, samples = table.shape
    half, total, cols = first.shape
    count = last.shape[1]
    skip = start // step
    return pl.pallas_call(
        inverse_kernel,
        grid=(count // step,),
        in_specs=[
            pl.BlockSpec((bins, samples), lambda i: (0, 0)),
            pl.BlockSpec((half, step, cols), lambda i: (0, i + skip, 0)),
            pl.BlockSpec((bins - half, step, cols), lambda i: (0, i, 0)),
        ]
        + ([] if prior is None else [pl.BlockSpec(memory_space=pl.ANY)]),
        out_specs=pl.BlockSpec((step, cols, samples), lambda i: (i + skip, 0, 0)),
        out_shape=jax.ShapeDtypeStruct((total, cols, samples), jnp.bfloat16),
        input_output_aliases={} if prior is None else {3: 0},
        cost_estimate=pl.CostEstimate(
            flops=2 * bins * samples * count * cols,
            bytes_accessed=2 * count * cols * (samples + bins),
            transcendentals=0,
        ),
        name="inverse_table",
    )(table, first, last, *([] if prior is None else [prior]))


def tri(value, other, upper):
    row = lax.broadcasted_iota(jnp.int32, value.shape, 0)
    col = lax.broadcasted_iota(jnp.int32, value.shape, 1)
    return jnp.where(row <= col, value, other) if upper else jnp.where(row > col, value, other)


def diagonal(value):
    row = lax.broadcasted_iota(jnp.int32, value.shape, 0)
    col = lax.broadcasted_iota(jnp.int32, value.shape, 1)
    return jnp.sum(jnp.where(row == col, value, 0.0), axis=0, keepdims=True)


def with_diagonal(value, line):
    row = lax.broadcasted_iota(jnp.int32, value.shape, 0)
    col = lax.broadcasted_iota(jnp.int32, value.shape, 1)
    return jnp.where(row == col, jnp.broadcast_to(line, value.shape), value)


EXTRA = 8


def fold_kernel(place_ref, whole_ref, swap_ref, *refs):
    *hand_refs, out_ref = refs
    count, length, cols = whole_ref.shape
    piece = hand_refs[0].shape[1]
    kept = length - piece
    diagonal_device, side = place_ref[0], place_ref[1]

    def each(d, carry):
        @pl.when(diagonal_device == 1)
        def _():
            for half in range(2):
                real = whole_ref[d, half * cols : (half + 1) * cols].astype(jnp.float32)
                imag = whole_ref[d, (2 + half) * cols : (3 + half) * cols].astype(jnp.float32)
                span = slice(half * cols, (half + 1) * cols)

                @pl.when(side == half)
                def _():
                    mean_real = 0.5 * (real + real.T)
                    mean_imag = 0.5 * (imag + imag.T)
                    out_ref[d, span] = tri(mean_real, mean_imag, True).astype(out_ref.dtype)
                    line = jnp.broadcast_to(diagonal(mean_imag), (EXTRA, cols))
                    out_ref[d, kept:] = line.astype(out_ref.dtype)

                @pl.when(side != half)
                def _():
                    own = imag if half else real
                    mean = 0.5 * (own + swap_ref[d].astype(jnp.float32).T)
                    out_ref[d, span] = mean.astype(out_ref.dtype)

            for index, hand_ref in enumerate(hand_refs):
                start = 2 * cols + index * piece
                out_ref[d, start : start + piece] = hand_ref[d]

        @pl.when(diagonal_device == 0)
        def _():
            out_ref[d, :kept] = whole_ref[d, :kept]
            out_ref[d, kept:] = jnp.zeros((EXTRA, cols), out_ref.dtype)

        return carry

    lax.fori_loop(0, count, each, 0)


def unfold_kernel(place_ref, folded_ref, swap_ref, *refs):
    *hand_refs, out_ref = refs
    count, length, cols = out_ref.shape
    piece = hand_refs[0].shape[1]
    kept = length - piece
    diagonal_device, side, turn = place_ref[0], place_ref[1], place_ref[2]

    def each(d, carry):
        @pl.when(diagonal_device == 1)
        def _():
            for half in range(2):
                own = folded_ref[d, half * cols : (half + 1) * cols]
                real = slice(half * cols, (half + 1) * cols)
                imag = slice((2 + half) * cols, (3 + half) * cols)

                @pl.when(side == half)
                def _():
                    packed = own.astype(jnp.float32)
                    line = folded_ref[d, kept:].astype(jnp.float32)[:1]
                    out_ref[d, real] = tri(packed, packed.T, True).astype(out_ref.dtype)
                    lower = with_diagonal(tri(packed, packed.T, False), line)
                    out_ref[d, imag] = lower.astype(out_ref.dtype)

                @pl.when(side != half)
                def _():
                    other = swap_ref[d].astype(jnp.float32).T.astype(out_ref.dtype)
                    out_ref[d, imag if half else real] = own
                    out_ref[d, real if half else imag] = other

        @pl.when(diagonal_device == 0)
        def _():
            out_ref[d, :kept] = folded_ref[d, :kept]

            for index, hand_ref in enumerate(hand_refs):

                @pl.when(turn == index + 1)
                def _():
                    out_ref[d, kept:] = hand_ref[d]

        return carry

    lax.fori_loop(0, count, each, 0)


def per_device(kernel, place, first, swap, hands, shape, name, step=4):
    devices = first.shape[0]

    def spec(array_shape):
        rest = len(array_shape) - 1
        return pl.BlockSpec((step,) + tuple(array_shape[1:]), lambda i: (i,) + (0,) * rest)

    return pl.pallas_call(
        kernel,
        grid=(devices // step,),
        in_specs=[pl.BlockSpec(memory_space=pltpu.SMEM)]
        + [spec(a.shape) for a in (first, swap, *hands)],
        out_specs=spec(shape),
        out_shape=jax.ShapeDtypeStruct(shape, first.dtype),
        cost_estimate=pl.CostEstimate(
            flops=4 * first.size, bytes_accessed=8 * first.size, transcendentals=0
        ),
        name=name,
    )(place, first, swap, *hands)


def owner_kernel(wave_ref, recv_ref, *refs, sources, groups, cols, fold_in, fold_out):
    out_refs, (held, done) = refs[:-2], refs[-2:]
    out_ref = out_refs[0]
    halves = groups // sources
    rows = halves * cols
    piece = cols // 2
    kept = 2 * rows - piece

    def at(block):
        return pl.ds(pl.multiple_of(block * cols, cols), cols)

    def load(d, start):
        return recv_ref[d, start * cols : (start + 1) * cols].astype(jnp.float32)

    def slot(turn):
        return slice(2 * cols + (turn - 1) * piece, 2 * cols + turn * piece)

    def load_kept(part, half, src, col, owner_src, turn):
        if part == 0 or half == 0:
            return load(src * groups + col, part * halves + half)
        upper = recv_ref[src * groups + col, kept - piece : kept].astype(jnp.float32)
        lower = recv_ref[owner_src * groups + col, slot(turn)].astype(jnp.float32)
        return jnp.concatenate([upper, lower], 0)

    def put(part, row, col, value):
        held[part, at(row), at(col)] = value.astype(jnp.bfloat16)

    def mirror_whole(src, carry):
        for half in range(halves):
            block = src * halves + half
            for part in range(2):
                for col in range(groups):
                    a = load(src * groups + col, part * halves + half)
                    b = load((col // halves) * groups + block, part * halves + col % halves)
                    put(part, block, col, 0.5 * (a + b.T))
        return carry

    def mirror_folded(src, carry):
        for turn in range(1, sources):
            other = src ^ turn
            for half in range(halves):
                row = src * halves + half
                for side in range(halves):
                    col = other * halves + side
                    for part in range(2):
                        a = load_kept(part, half, src, col, other, turn)
                        b = load_kept(part, side, other, row, src, turn)
                        put(part, row, col, 0.5 * (a + b.T))
        low, high = src * halves, src * halves + 1
        for side in range(halves):
            block = src * halves + side
            d = src * groups + block
            packed = load(d, side)
            line = recv_ref[d, kept:].astype(jnp.float32)[:1]
            put(0, block, block, tri(packed, packed.T, True))
            put(1, block, block, with_diagonal(tri(packed, packed.T, False), line))
        real = load(src * groups + high, 0)
        imag = load(src * groups + low, 1)
        put(0, low, high, real)
        put(0, high, low, real.T)
        put(1, high, low, imag)
        put(1, low, high, imag.T)
        return carry

    lax.fori_loop(0, sources, mirror_folded if fold_in else mirror_whole, 0)

    wave_real, wave_imag = wave_ref[0], wave_ref[1]
    two_real = wave_real * wave_real - wave_imag * wave_imag
    two_imag = 2.0 * wave_real * wave_imag

    def dot(left, right):
        return jnp.dot(left, right, preferred_element_type=jnp.float32)

    def product(src, carry):
        span = pl.ds(pl.multiple_of(src * rows, rows), rows)
        real, imag = held[0, span, :], held[1, span, :]
        sq_real = dot(real, held[0]) - dot(imag, held[1])
        sq_imag = dot(real, held[1]) + dot(imag, held[0])
        out_real = real.astype(jnp.float32) - (wave_real * sq_real - wave_imag * sq_imag)
        out_imag = imag.astype(jnp.float32) - (wave_real * sq_imag + wave_imag * sq_real)
        left_real, left_imag = sq_real.astype(jnp.bfloat16), sq_imag.astype(jnp.bfloat16)
        cube_real = dot(left_real, held[0]) - dot(left_imag, held[1])
        cube_imag = dot(left_real, held[1]) + dot(left_imag, held[0])
        out_real = (out_real + (two_real * cube_real - two_imag * cube_imag)).astype(jnp.bfloat16)
        out_imag = (out_imag + (two_real * cube_imag + two_imag * cube_real)).astype(jnp.bfloat16)
        if fold_out:
            done[0, span, :] = out_real
            done[1, span, :] = out_imag
        else:
            top = out_refs[0].shape[1] // 2
            for col in range(groups):
                for part, value in enumerate((out_real, out_imag)):
                    tile = value[:, col * cols : (col + 1) * cols]
                    d = src * groups + col
                    out_refs[0][d, part * top : (part + 1) * top] = tile[:top]
                    out_refs[1][d, part * (rows - top) : (part + 1) * (rows - top)] = tile[top:]
        return carry

    lax.fori_loop(0, sources, product, 0)
    if not fold_out:
        return

    def pack(src, carry):
        span = pl.ds(pl.multiple_of(src * rows, rows), rows)
        for turn in range(1, sources):
            other = src ^ turn
            for side in range(halves):
                col = other * halves + side
                d = src * groups + col
                imag = done[1, span, at(col)]
                out_ref[d, :rows] = done[0, span, at(col)]
                out_ref[d, rows:kept] = imag[: rows - piece]
                out_ref[d, kept:] = jnp.zeros((EXTRA, cols), jnp.bfloat16)
                out_ref[other * groups + col, slot(turn)] = imag[rows - piece :]
        for side in range(halves):
            block = src * halves + side
            d = src * groups + block
            real = done[0, at(block), at(block)].astype(jnp.float32)
            imag = done[1, at(block), at(block)].astype(jnp.float32)
            out_ref[d, side * cols : (side + 1) * cols] = tri(real, imag, True).astype(jnp.bfloat16)
            line = jnp.broadcast_to(diagonal(imag), (EXTRA, cols))
            out_ref[d, kept:] = line.astype(jnp.bfloat16)
        low, high = src * halves, src * halves + 1
        out_ref[src * groups + high, :cols] = done[0, at(low), at(high)]
        out_ref[src * groups + low, cols : 2 * cols] = done[1, at(high), at(low)]
        return carry

    lax.fori_loop(0, sources, pack, 0)


def owner(wave, recv, sources, groups, fold_in, fold_out):
    devices, _, cols = recv.shape
    total = groups * cols
    whole = 2 * (total // sources)
    lengths = [whole - cols // 2 + EXTRA] if fold_out else [whole - 2 * EDGE, 2 * EDGE]
    return pl.pallas_call(
        functools.partial(
            owner_kernel,
            sources=sources,
            groups=groups,
            cols=cols,
            fold_in=fold_in,
            fold_out=fold_out,
        ),
        in_specs=[
            pl.BlockSpec(memory_space=pltpu.SMEM),
            pl.BlockSpec(memory_space=pltpu.VMEM),
        ],
        out_specs=[pl.BlockSpec(memory_space=pltpu.VMEM)] * len(lengths),
        out_shape=[jax.ShapeDtypeStruct((devices, n, cols), recv.dtype) for n in lengths],
        scratch_shapes=[
            pltpu.VMEM((2, total, total), jnp.bfloat16),
            pltpu.VMEM((2, total, total) if fold_out else (2, 16, 128), jnp.bfloat16),
        ],
        cost_estimate=pl.CostEstimate(
            flops=16 * total**3,
            bytes_accessed=8 * devices * whole * cols,
            transcendentals=0,
        ),
        compiler_params=pltpu.CompilerParams(vmem_limit_bytes=56 << 20),
        name="owned_frequency",
    )(wave, recv)


AXES = ("src", "rcv")


def swap_pairs(sources, groups):
    halves = groups // sources
    return [
        (src * groups + src * halves + side, src * groups + src * halves + 1 - side)
        for src in range(sources)
        for side in range(halves)
    ]


def hand_pairs(sources, groups, turn, back):
    pairs = []
    for col in range(groups):
        src = col // (groups // sources)
        pair = ((src ^ turn) * groups + col, src * groups + col)
        pairs.append(pair[::-1] if back else pair)
    return pairs


def where_am_i(sources, groups):
    halves = groups // sources
    src, col = lax.axis_index("src"), lax.axis_index("rcv")
    turn = src ^ (col // halves)
    return turn, col % halves


def fold(spectra, sources, groups):
    devices, length, cols = spectra.shape
    piece = cols // 2
    turn, side = where_am_i(sources, groups)
    block = lax.dynamic_slice_in_dim(spectra, jnp.where(side == 0, 1, 2) * cols, cols, 1)
    swap = lax.ppermute(block, AXES, swap_pairs(sources, groups))
    last = spectra[:, length - piece :]
    hands = [
        lax.ppermute(last, AXES, hand_pairs(sources, groups, t, False)) for t in range(1, sources)
    ]
    place = jnp.stack([(turn == 0).astype(jnp.int32), side, turn]).astype(jnp.int32)
    shape = (devices, length - piece + EXTRA, cols)
    return per_device(fold_kernel, place, spectra, swap, hands, shape, "fold")


def unfold(folded, sources, groups):
    devices, length, cols = folded.shape
    piece = cols // 2
    turn, side = where_am_i(sources, groups)
    block = lax.dynamic_slice_in_dim(folded, (1 - side) * cols, cols, 1)
    swap = lax.ppermute(block, AXES, swap_pairs(sources, groups))
    hands = []
    for t in range(1, sources):
        start = 2 * cols + (t - 1) * piece
        pairs = hand_pairs(sources, groups, t, True)
        hands.append(lax.ppermute(folded[:, start : start + piece], AXES, pairs))
    place = jnp.stack([(turn == 0).astype(jnp.int32), side, turn]).astype(jnp.int32)
    shape = (devices, length - EXTRA + piece, cols)
    return per_device(unfold_kernel, place, folded, swap, hands, shape, "unfold")


def exchange(array):
    return lax.all_to_all(array, AXES, 0, 0, tiled=True)


def local_whole(wavefield, inverse_wavelet):
    src_rows, rcv_cols, samples = wavefield.shape
    count_f = inverse_wavelet.shape[1]
    sources, groups = lax.axis_size("src"), lax.axis_size("rcv")
    devices = sources * groups
    me = lax.axis_index(AXES)
    forward, inverse = tables(samples, count_f, F0)
    width = 2 * devices
    wavelets = [
        lax.dynamic_index_in_dim(inverse_wavelet, start + me, 1, keepdims=False)
        for start in range(0, count_f, devices)
    ]

    def spectra(chunk, start, count, step):
        rows = dft(forward[chunk * width : (chunk + 1) * width], wavefield, start, count, step)
        return rows.reshape(devices, 2 * count, rcv_cols)

    plain = exchange(spectra(0, 0, src_rows, 2 * EDGE))
    folded = exchange(fold(spectra(1, 0, src_rows, 2 * EDGE), sources, groups))
    (cleaned,) = owner(wavelets[0], plain, sources, groups, False, True)
    first = unfold(exchange(cleaned), sources, groups).reshape(width, src_rows, rcv_cols)
    most, rest = owner(wavelets[1], folded, sources, groups, True, False)
    most, rest, first = lax.optimization_barrier((exchange(most), rest, first))
    rest = exchange(rest)
    most = most.reshape(width, src_rows - EDGE, rcv_cols)
    rest = rest.reshape(width, EDGE, rcv_cols)
    out = inverse_rows(inverse, first, most, 0, EDGE)
    return inverse_rows(inverse, first, rest, src_rows - EDGE, EDGE, out)


def solution(mesh):
    placed = (P("src", "rcv", None), P())

    def local(wavefield, inverse_wavelet):
        sources, groups = lax.axis_size("src"), lax.axis_size("rcv")
        fits = inverse_wavelet.shape[1] == 2 * sources * groups
        if fits and sources == 4 and groups == 2 * sources:
            return local_whole(wavefield, inverse_wavelet)
        return local_sliced(wavefield, inverse_wavelet)

    return jax.shard_map(
        local, mesh=mesh, in_specs=placed, out_specs=P("src", "rcv", None), check_vma=False
    )
```

```python
import functools
import math

import jax
import jax.numpy as jnp
from jax import lax
from jax.experimental import pallas as pl
from jax.experimental.pallas import tpu as pltpu
from jax.sharding import PartitionSpec as P

F0 = 8


def tables(count_t, count_f, first):
    times = jnp.arange(count_t, dtype=jnp.int32)
    freqs = first + jnp.arange(count_f, dtype=jnp.int32)
    phase = freqs[:, None] * times[None, :] % count_t
    angle = phase.astype(jnp.float32) * (2.0 * math.pi / count_t)
    rows = jnp.stack([jnp.cos(angle), -jnp.sin(angle)], 1).reshape(2 * count_f, count_t)
    forward = (rows / math.sqrt(count_t)).astype(jnp.bfloat16)
    inverse = (rows / math.sqrt(count_f)).astype(jnp.bfloat16)
    return (forward, inverse)


def combine(mirror_real, mirror_imag, sq_real, sq_imag, cube_real, cube_imag, wave_real, wave_imag):
    two_real = wave_real * wave_real - wave_imag * wave_imag
    two_imag = 2.0 * wave_real * wave_imag
    out_real = (
        mirror_real
        - (wave_real * sq_real - wave_imag * sq_imag)
        + (two_real * cube_real - two_imag * cube_imag)
    )
    out_imag = (
        mirror_imag
        - (wave_real * sq_imag + wave_imag * sq_real)
        + (two_real * cube_imag + two_imag * cube_real)
    )
    return (out_real, out_imag)


def multiply(left_side, right_side):
    return jnp.einsum("fmk,fkn->fmn", left_side, right_side, preferred_element_type=jnp.float32)


def complex_product(left_side, right_side):
    real_part = multiply(left_side[:, 0], right_side[:, 0]) - multiply(
        left_side[:, 1], right_side[:, 1]
    )
    imag_part = multiply(left_side[:, 0], right_side[:, 1]) + multiply(
        left_side[:, 1], right_side[:, 0]
    )
    return (real_part, imag_part)


def local_sliced(wavefield, inverse_wavelet):
    src_rows, rcv_cols, samples = wavefield.shape
    count_f = inverse_wavelet.shape[1]
    groups = lax.axis_size("rcv")
    per_dev = count_f // groups
    forward, inverse = tables(samples, count_f, F0)
    spectra = jnp.einsum(
        "ct,srt->csr", forward, wavefield, preferred_element_type=jnp.float32
    ).astype(jnp.bfloat16)
    spectra = spectra.reshape(groups, 2 * per_dev, src_rows, rcv_cols)
    slices = lax.all_to_all(spectra, "rcv", split_axis=0, concat_axis=3, tiled=True)
    total_cols = slices.shape[3]
    slices = slices.reshape(per_dev, 2, src_rows, total_cols)
    whole = lax.all_gather(slices, "src", axis=2, tiled=True).astype(jnp.float32)
    all_rows = (0.5 * (whole + jnp.swapaxes(whole, 2, 3))).astype(jnp.bfloat16)
    mirrored = lax.dynamic_slice_in_dim(all_rows, lax.axis_index("src") * src_rows, src_rows, 2)
    sq_real, sq_imag = complex_product(mirrored, all_rows)
    squared = jnp.stack([sq_real, sq_imag], 1).astype(jnp.bfloat16)
    cube_real, cube_imag = complex_product(squared, all_rows)
    wavelet = lax.dynamic_slice_in_dim(inverse_wavelet, lax.axis_index("rcv") * per_dev, per_dev, 1)
    wave_real = wavelet[0][:, None, None]
    wave_imag = wavelet[1][:, None, None]
    out_real, out_imag = combine(
        mirrored[:, 0].astype(jnp.float32),
        mirrored[:, 1].astype(jnp.float32),
        sq_real,
        sq_imag,
        cube_real,
        cube_imag,
        wave_real,
        wave_imag,
    )
    cleaned = (
        jnp.stack([out_real, out_imag], 1)
        .astype(jnp.bfloat16)
        .reshape(1, 2 * per_dev, src_rows, total_cols)
    )
    returned = lax.all_to_all(cleaned, "rcv", split_axis=3, concat_axis=0, tiled=True)
    returned = returned.reshape(2 * count_f, src_rows, rcv_cols)
    return jnp.einsum("csr,ct->srt", returned, inverse, preferred_element_type=jnp.float32).astype(
        jnp.bfloat16
    )


NT_DIMS = (((1,), (1,)), ((), ()))
TN_DIMS = (((0,), (0,)), ((), ()))
EDGE = 32


def dft_kernel(table_ref, wave_ref, out_ref, *, group):
    rows, cols, samples = wave_ref.shape
    for first in range(0, rows, group):
        flat = wave_ref[first : first + group].reshape(group * cols, samples)
        values = lax.dot_general(flat, table_ref[...], NT_DIMS, preferred_element_type=jnp.float32)
        turned = [values[row * cols : (row + 1) * cols].T for row in range(group)]
        stacked = jnp.swapaxes(jnp.stack(turned, 0), 0, 1)
        out_ref[:, first : first + group, :] = stacked.astype(out_ref.dtype)


def dft(table, wave, start, count, step):
    _, cols, samples = wave.shape
    bins = table.shape[0]
    skip = start // step
    return pl.pallas_call(
        functools.partial(dft_kernel, group=16),
        grid=(count // step,),
        in_specs=[
            pl.BlockSpec((bins, samples), lambda i: (0, 0)),
            pl.BlockSpec((step, cols, samples), lambda i: (i + skip, 0, 0)),
        ],
        out_specs=pl.BlockSpec((bins, step, cols), lambda i: (0, i, 0)),
        out_shape=jax.ShapeDtypeStruct((bins, count, cols), jnp.bfloat16),
        cost_estimate=pl.CostEstimate(
            flops=2 * bins * samples * count * cols,
            bytes_accessed=2 * count * cols * (samples + bins),
            transcendentals=0,
        ),
        name="forward_table",
    )(table, wave)


def inverse_kernel(table_ref, first_ref, last_ref, *refs):
    out_ref = refs[-1]
    table = table_ref[...]
    both = jnp.swapaxes(jnp.concatenate([first_ref[...], last_ref[...]], 0), 0, 1)
    for row in range(out_ref.shape[0]):
        out_ref[row] = lax.dot_general(
            both[row], table, TN_DIMS, preferred_element_type=jnp.float32
        ).astype(out_ref.dtype)


def inverse_rows(table, first, last, start, step, prior=None):
    bins, samples = table.shape
    half, total, cols = first.shape
    count = last.shape[1]
    skip = start // step
    return pl.pallas_call(
        inverse_kernel,
        grid=(count // step,),
        in_specs=[
            pl.BlockSpec((bins, samples), lambda i: (0, 0)),
            pl.BlockSpec((half, step, cols), lambda i: (0, i + skip, 0)),
            pl.BlockSpec((bins - half, step, cols), lambda i: (0, i, 0)),
        ]
        + ([] if prior is None else [pl.BlockSpec(memory_space=pl.ANY)]),
        out_specs=pl.BlockSpec((step, cols, samples), lambda i: (i + skip, 0, 0)),
        out_shape=jax.ShapeDtypeStruct((total, cols, samples), jnp.bfloat16),
        input_output_aliases={} if prior is None else {3: 0},
        cost_estimate=pl.CostEstimate(
            flops=2 * bins * samples * count * cols,
            bytes_accessed=2 * count * cols * (samples + bins),
            transcendentals=0,
        ),
        name="inverse_table",
    )(table, first, last, *([] if prior is None else [prior]))


def tri(value, other, upper):
    row = lax.broadcasted_iota(jnp.int32, value.shape, 0)
    col = lax.broadcasted_iota(jnp.int32, value.shape, 1)
    return jnp.where(row <= col, value, other) if upper else jnp.where(row > col, value, other)


def diagonal(value):
    row = lax.broadcasted_iota(jnp.int32, value.shape, 0)
    col = lax.broadcasted_iota(jnp.int32, value.shape, 1)
    return jnp.sum(jnp.where(row == col, value, 0.0), axis=0, keepdims=True)


def with_diagonal(value, line):
    row = lax.broadcasted_iota(jnp.int32, value.shape, 0)
    col = lax.broadcasted_iota(jnp.int32, value.shape, 1)
    return jnp.where(row == col, jnp.broadcast_to(line, value.shape), value)


EXTRA = 8


def fold_kernel(place_ref, whole_ref, swap_ref, two_ref, three_ref, last_ref, out_ref):
    count, length, cols = whole_ref.shape
    kept = out_ref.shape[1] - EXTRA
    turn, side, lower = place_ref[0], place_ref[1], place_ref[2]

    def plane(d, part, half):
        start = (2 * part + half) * cols
        return whole_ref[d, start : start + cols]

    def each(d, carry):
        @pl.when(turn == 0)
        def _():
            for half in range(2):
                real = plane(d, 0, half).astype(jnp.float32)
                imag = plane(d, 1, half).astype(jnp.float32)
                span = slice(half * cols, (half + 1) * cols)

                @pl.when(side == half)
                def _():
                    mean_real = 0.5 * (real + real.T)
                    mean_imag = 0.5 * (imag + imag.T)
                    out_ref[d, span] = tri(mean_real, mean_imag, True).astype(out_ref.dtype)
                    line = jnp.broadcast_to(diagonal(mean_imag), (EXTRA, cols))
                    out_ref[d, kept:] = line.astype(out_ref.dtype)

                @pl.when(side != half)
                def _():
                    own = imag if half else real
                    mean = 0.5 * (own + swap_ref[d].astype(jnp.float32).T)
                    out_ref[d, span] = mean.astype(out_ref.dtype)

            middle = 2 * cols + two_ref.shape[1]
            out_ref[d, 2 * cols : middle] = two_ref[d]
            out_ref[d, middle:kept] = three_ref[d]

        @pl.when(turn == 1)
        def _():
            for half in range(2):

                @pl.when(side == half)
                def _():
                    own = jnp.where(lower == 1, plane(d, 0, half), plane(d, 1, half))
                    mean = 0.5 * (own.astype(jnp.float32) + swap_ref[d].astype(jnp.float32).T)
                    out_ref[d, :cols] = mean.astype(out_ref.dtype)

                @pl.when(side != half)
                def _():
                    out_ref[d, cols : 2 * cols] = plane(d, 0, half)
                    out_ref[d, 2 * cols : 3 * cols] = plane(d, 1, half)

            out_ref[d, 3 * cols : kept] = last_ref[d]
            out_ref[d, kept:] = jnp.zeros((EXTRA, cols), out_ref.dtype)

        @pl.when(turn > 1)
        def _():
            out_ref[d, :kept] = whole_ref[d, :kept]
            out_ref[d, kept:] = jnp.zeros((EXTRA, cols), out_ref.dtype)

        return carry

    lax.fori_loop(0, count, each, 0)


def unfold_kernel(place_ref, folded_ref, swap_ref, two_ref, three_ref, last_ref, out_ref):
    count, length, cols = out_ref.shape
    kept = folded_ref.shape[1] - EXTRA
    turn, side, lower = place_ref[0], place_ref[1], place_ref[2]

    def each(d, carry):
        @pl.when(turn == 0)
        def _():
            for half in range(2):
                own = folded_ref[d, half * cols : (half + 1) * cols]
                real = slice(half * cols, (half + 1) * cols)
                imag = slice((2 + half) * cols, (3 + half) * cols)

                @pl.when(side == half)
                def _():
                    packed = own.astype(jnp.float32)
                    line = folded_ref[d, kept:].astype(jnp.float32)[:1]
                    out_ref[d, real] = tri(packed, packed.T, True).astype(out_ref.dtype)
                    below = with_diagonal(tri(packed, packed.T, False), line)
                    out_ref[d, imag] = below.astype(out_ref.dtype)

                @pl.when(side != half)
                def _():
                    other = swap_ref[d].astype(jnp.float32).T.astype(out_ref.dtype)
                    out_ref[d, imag if half else real] = own
                    out_ref[d, real if half else imag] = other

        @pl.when(turn == 1)
        def _():
            for half in range(2):
                real = slice(half * cols, (half + 1) * cols)
                imag = slice((2 + half) * cols, (3 + half) * cols)

                @pl.when(side == half)
                def _():
                    own = folded_ref[d, :cols]
                    other = swap_ref[d].astype(jnp.float32).T.astype(out_ref.dtype)
                    out_ref[d, real] = jnp.where(lower == 1, own, other)
                    out_ref[d, imag] = jnp.where(lower == 1, other, own)

                @pl.when(side != half)
                def _():
                    out_ref[d, real] = folded_ref[d, cols : 2 * cols]
                    out_ref[d, imag] = folded_ref[d, 2 * cols : 3 * cols]

        @pl.when(turn > 1)
        def _():
            out_ref[d, :kept] = folded_ref[d, :kept]

        @pl.when(turn == 2)
        def _():
            out_ref[d, kept:] = two_ref[d]

        @pl.when(turn == 3)
        def _():
            middle = kept + three_ref.shape[1]
            out_ref[d, kept:middle] = three_ref[d]
            out_ref[d, middle:] = last_ref[d]

        return carry

    lax.fori_loop(0, count, each, 0)


def per_device(kernel, place, first, swap, hands, shape, name, step=8):
    devices = first.shape[0]

    def spec(array_shape):
        rest = len(array_shape) - 1
        return pl.BlockSpec((step,) + tuple(array_shape[1:]), lambda i: (i,) + (0,) * rest)

    return pl.pallas_call(
        kernel,
        grid=(devices // step,),
        in_specs=[pl.BlockSpec(memory_space=pltpu.SMEM)]
        + [spec(a.shape) for a in (first, swap, *hands)],
        out_specs=spec(shape),
        out_shape=jax.ShapeDtypeStruct(shape, first.dtype),
        cost_estimate=pl.CostEstimate(
            flops=4 * first.size, bytes_accessed=8 * first.size, transcendentals=0
        ),
        name=name,
    )(place, first, swap, *hands)


def owner_kernel(wave_ref, recv_ref, *refs, sources, groups, cols, fold_in, fold_out):
    out_refs, (held, done) = refs[:-2], refs[-2:]
    out_ref = out_refs[0]
    halves = groups // sources
    rows = halves * cols
    quarter = cols // 4
    kept = 3 * cols + quarter

    def at(block):
        return pl.ds(pl.multiple_of(block * cols, cols), cols)

    def load(d, start):
        return recv_ref[d, start * cols : (start + 1) * cols].astype(jnp.float32)

    def moved(src, col, turn):
        two, three = 2 * cols, 2 * cols + 3 * quarter
        if turn == 2:
            return [(src * groups + col, two, three)]
        return [
            (src * groups + col, three, kept),
            ((src ^ 1) * groups + col, 3 * cols, kept),
        ]

    def load_kept(part, half, src, col, owner_src, turn):
        if part == 0 or half == 0:
            return load(src * groups + col, part * halves + half)
        spans = [(src * groups + col, 3 * cols, kept)] + moved(owner_src, col, turn)
        return jnp.concatenate(
            [recv_ref[d, start:stop].astype(jnp.float32) for d, start, stop in spans], 0
        )

    def put(part, row, col, value):
        held[part, at(row), at(col)] = value.astype(jnp.bfloat16)

    def mirror_whole(src, carry):
        for half in range(halves):
            block = src * halves + half
            for part in range(2):
                for col in range(groups):
                    a = load(src * groups + col, part * halves + half)
                    b = load((col // halves) * groups + block, part * halves + col % halves)
                    put(part, block, col, 0.5 * (a + b.T))
        return carry

    def mirror_folded(src, carry):
        for turn in range(2, sources):
            other = src ^ turn
            for half in range(halves):
                row = src * halves + half
                for side in range(halves):
                    col = other * halves + side
                    for part in range(2):
                        a = load_kept(part, half, src, col, other, turn)
                        b = load_kept(part, side, other, row, src, turn)
                        put(part, row, col, 0.5 * (a + b.T))
        low, high = src * halves, src * halves + 1
        for side in range(halves):
            block = src * halves + side
            d = src * groups + block
            packed = load(d, side)
            line = recv_ref[d, kept:].astype(jnp.float32)[:1]
            put(0, block, block, tri(packed, packed.T, True))
            put(1, block, block, with_diagonal(tri(packed, packed.T, False), line))
        real = load(src * groups + high, 0)
        imag = load(src * groups + low, 1)
        put(0, low, high, real)
        put(0, high, low, real.T)
        put(1, high, low, imag)
        put(1, low, high, imag.T)
        return carry

    def mirror_near(pair, carry):
        low, high = 2 * pair, 2 * pair + 1
        for half in range(halves):
            row, col = low * halves + half, high * halves + half
            real = load(low * groups + col, 0)
            imag = load(high * groups + row, 0)
            put(0, row, col, real)
            put(0, col, row, real.T)
            put(1, col, row, imag)
            put(1, row, col, imag.T)
            col = high * halves + 1 - half
            for part in range(2):
                a = load(low * groups + col, 1 + part)
                b = load(high * groups + row, 1 + part)
                mean = 0.5 * (a + b.T)
                put(part, row, col, mean)
                put(part, col, row, mean.T)
        return carry

    if fold_in:
        lax.fori_loop(0, sources, mirror_folded, 0)
        lax.fori_loop(0, sources // 2, mirror_near, 0)
    else:
        lax.fori_loop(0, sources, mirror_whole, 0)

    wave_real, wave_imag = wave_ref[0], wave_ref[1]
    two_real = wave_real * wave_real - wave_imag * wave_imag
    two_imag = 2.0 * wave_real * wave_imag

    def dot(left, right):
        return jnp.dot(left, right, preferred_element_type=jnp.float32)

    def product(src, carry):
        span = pl.ds(pl.multiple_of(src * rows, rows), rows)
        real, imag = held[0, span, :], held[1, span, :]
        sq_real = dot(real, held[0]) - dot(imag, held[1])
        sq_imag = dot(real, held[1]) + dot(imag, held[0])
        out_real = real.astype(jnp.float32) - (wave_real * sq_real - wave_imag * sq_imag)
        out_imag = imag.astype(jnp.float32) - (wave_real * sq_imag + wave_imag * sq_real)
        left_real, left_imag = sq_real.astype(jnp.bfloat16), sq_imag.astype(jnp.bfloat16)
        cube_real = dot(left_real, held[0]) - dot(left_imag, held[1])
        cube_imag = dot(left_real, held[1]) + dot(left_imag, held[0])
        out_real = (out_real + (two_real * cube_real - two_imag * cube_imag)).astype(jnp.bfloat16)
        out_imag = (out_imag + (two_real * cube_imag + two_imag * cube_real)).astype(jnp.bfloat16)
        if fold_out:
            done[0, span, :] = out_real
            done[1, span, :] = out_imag
        else:
            top = out_refs[0].shape[1] // 2
            for col in range(groups):
                for part, value in enumerate((out_real, out_imag)):
                    tile = value[:, col * cols : (col + 1) * cols]
                    d = src * groups + col
                    out_refs[0][d, part * top : (part + 1) * top] = tile[:top]
                    out_refs[1][d, part * (rows - top) : (part + 1) * (rows - top)] = tile[top:]
        return carry

    lax.fori_loop(0, sources, product, 0)
    if not fold_out:
        return

    def pack(src, carry):
        span = pl.ds(pl.multiple_of(src * rows, rows), rows)
        for turn in range(2, sources):
            other = src ^ turn
            for side in range(halves):
                col = other * halves + side
                d = src * groups + col
                imag = done[1, span, at(col)]
                out_ref[d, :rows] = done[0, span, at(col)]
                out_ref[d, rows:kept] = imag[: kept - rows]
                out_ref[d, kept:] = jnp.zeros((EXTRA, cols), jnp.bfloat16)
                first = kept - rows
                for place, start, stop in moved(other, col, turn):
                    out_ref[place, start:stop] = imag[first : first + stop - start]
                    first += stop - start
        for side in range(halves):
            block = src * halves + side
            d = src * groups + block
            real = done[0, at(block), at(block)].astype(jnp.float32)
            imag = done[1, at(block), at(block)].astype(jnp.float32)
            out_ref[d, side * cols : (side + 1) * cols] = tri(real, imag, True).astype(jnp.bfloat16)
            line = jnp.broadcast_to(diagonal(imag), (EXTRA, cols))
            out_ref[d, kept:] = line.astype(jnp.bfloat16)
        low, high = src * halves, src * halves + 1
        out_ref[src * groups + high, :cols] = done[0, at(low), at(high)]
        out_ref[src * groups + low, cols : 2 * cols] = done[1, at(high), at(low)]
        return carry

    def pack_near(pair, carry):
        low, high = 2 * pair, 2 * pair + 1
        for half in range(halves):
            row, col = low * halves + half, high * halves + half
            out_ref[low * groups + col, :cols] = done[0, at(row), at(col)]
            out_ref[high * groups + row, :cols] = done[1, at(col), at(row)]
            col = high * halves + 1 - half
            for part in range(2):
                slot = slice((1 + part) * cols, (2 + part) * cols)
                out_ref[low * groups + col, slot] = done[part, at(row), at(col)]
                out_ref[high * groups + row, slot] = done[part, at(col), at(row)]
            for d in (low * groups + col, high * groups + row):
                out_ref[d, kept:] = jnp.zeros((EXTRA, cols), jnp.bfloat16)
        return carry

    lax.fori_loop(0, sources, pack, 0)
    lax.fori_loop(0, sources // 2, pack_near, 0)


def owner(wave, recv, sources, groups, fold_in, fold_out):
    devices, _, cols = recv.shape
    total = groups * cols
    whole = 2 * (total // sources)
    lengths = [3 * cols + cols // 4 + EXTRA] if fold_out else [whole - 2 * EDGE, 2 * EDGE]
    return pl.pallas_call(
        functools.partial(
            owner_kernel,
            sources=sources,
            groups=groups,
            cols=cols,
            fold_in=fold_in,
            fold_out=fold_out,
        ),
        in_specs=[
            pl.BlockSpec(memory_space=pltpu.SMEM),
            pl.BlockSpec(memory_space=pltpu.VMEM),
        ],
        out_specs=[pl.BlockSpec(memory_space=pltpu.VMEM)] * len(lengths),
        out_shape=[jax.ShapeDtypeStruct((devices, n, cols), recv.dtype) for n in lengths],
        scratch_shapes=[
            pltpu.VMEM((2, total, total), jnp.bfloat16),
            pltpu.VMEM((2, total, total) if fold_out else (2, 16, 128), jnp.bfloat16),
        ],
        cost_estimate=pl.CostEstimate(
            flops=16 * total**3,
            bytes_accessed=8 * devices * whole * cols,
            transcendentals=0,
        ),
        compiler_params=pltpu.CompilerParams(vmem_limit_bytes=56 << 20),
        name="owned_frequency",
    )(wave, recv)


AXES = ("src", "rcv")


def swap_pairs(sources, groups):
    halves = groups // sources
    pairs = []
    for src in range(sources):
        for side in range(halves):
            here = src * groups + src * halves + side
            pairs.append((here, src * groups + src * halves + 1 - side))
            near = src ^ 1
            pairs.append(
                (near * groups + src * halves + side, src * groups + near * halves + side)
            )
    return pairs


def turn_pairs(sources, groups, start, stop):
    halves = groups // sources
    return [
        ((col // halves ^ start) * groups + col, (col // halves ^ stop) * groups + col)
        for col in range(groups)
    ]


def where_am_i(sources, groups):
    halves = groups // sources
    src, col = lax.axis_index("src"), lax.axis_index("rcv")
    turn, side = src ^ (col // halves), col % halves
    place = jnp.stack([turn, side, (src < col // halves).astype(jnp.int32)])
    return turn, side, place.astype(jnp.int32)


def send_rows(array, start, stop, pairs):
    return lax.ppermute(array[:, start:stop], AXES, pairs)


def fold(spectra, sources, groups):
    devices, length, cols = spectra.shape
    quarter = cols // 4
    kept = 3 * cols + quarter
    turn, side, place = where_am_i(sources, groups)
    diagonal_plane = jnp.where(side == 0, 1, 2)
    near_plane = jnp.where(place[2] == 1, 2 + side, side)
    plane = jnp.where(turn == 0, diagonal_plane, near_plane)
    block = lax.dynamic_slice_in_dim(spectra, plane * cols, cols, 1)
    swap = lax.ppermute(block, AXES, swap_pairs(sources, groups))
    hands = [
        send_rows(spectra, kept, length, turn_pairs(sources, groups, 2, 0)),
        send_rows(spectra, kept, kept + 2 * quarter, turn_pairs(sources, groups, 3, 0)),
        send_rows(spectra, kept + 2 * quarter, length, turn_pairs(sources, groups, 3, 1)),
    ]
    shape = (devices, kept + EXTRA, cols)
    return per_device(fold_kernel, place, spectra, swap, hands, shape, "fold")


def unfold(folded, sources, groups):
    devices, length, cols = folded.shape
    quarter = cols // 4
    kept = 3 * cols + quarter
    middle = 2 * cols + 3 * quarter
    turn, side, place = where_am_i(sources, groups)
    plane = jnp.where(turn == 0, 1 - side, 0)
    block = lax.dynamic_slice_in_dim(folded, plane * cols, cols, 1)
    swap = lax.ppermute(block, AXES, swap_pairs(sources, groups))
    hands = [
        send_rows(folded, 2 * cols, middle, turn_pairs(sources, groups, 0, 2)),
        send_rows(folded, middle, kept, turn_pairs(sources, groups, 0, 3)),
        send_rows(folded, 3 * cols, kept, turn_pairs(sources, groups, 1, 3)),
    ]
    shape = (devices, 4 * cols, cols)
    return per_device(unfold_kernel, place, folded, swap, hands, shape, "unfold")


def exchange(array):
    return lax.all_to_all(array, AXES, 0, 0, tiled=True)


def local_whole(wavefield, inverse_wavelet):
    src_rows, rcv_cols, samples = wavefield.shape
    count_f = inverse_wavelet.shape[1]
    sources, groups = lax.axis_size("src"), lax.axis_size("rcv")
    devices = sources * groups
    me = lax.axis_index(AXES)
    forward, inverse = tables(samples, count_f, F0)
    width = 2 * devices
    wavelets = [
        lax.dynamic_index_in_dim(inverse_wavelet, start + me, 1, keepdims=False)
        for start in range(0, count_f, devices)
    ]

    def spectra(chunk, start, count, step):
        rows = dft(forward[chunk * width : (chunk + 1) * width], wavefield, start, count, step)
        return rows.reshape(devices, 2 * count, rcv_cols)

    plain = exchange(spectra(0, 0, src_rows, 2 * EDGE))
    folded = exchange(fold(spectra(1, 0, src_rows, 2 * EDGE), sources, groups))
    (cleaned,) = owner(wavelets[0], plain, sources, groups, False, True)
    first = unfold(exchange(cleaned), sources, groups).reshape(width, src_rows, rcv_cols)
    most, rest = owner(wavelets[1], folded, sources, groups, True, False)
    most, rest, first = lax.optimization_barrier((exchange(most), rest, first))
    rest = exchange(rest)
    most = most.reshape(width, src_rows - EDGE, rcv_cols)
    rest = rest.reshape(width, EDGE, rcv_cols)
    out = inverse_rows(inverse, first, most, 0, EDGE)
    return inverse_rows(inverse, first, rest, src_rows - EDGE, EDGE, out)


def solution(mesh):
    placed = (P("src", "rcv", None), P())

    def local(wavefield, inverse_wavelet):
        sources, groups = lax.axis_size("src"), lax.axis_size("rcv")
        fits = inverse_wavelet.shape[1] == 2 * sources * groups
        if fits and sources == 4 and groups == 2 * sources:
            return local_whole(wavefield, inverse_wavelet)
        return local_sliced(wavefield, inverse_wavelet)

    return jax.shard_map(
        local, mesh=mesh, in_specs=placed, out_specs=P("src", "rcv", None), check_vma=False
    )
```

```python
import functools
import math

import jax
import jax.numpy as jnp
from jax import lax
from jax.experimental import pallas as pl
from jax.experimental.pallas import tpu as pltpu
from jax.sharding import PartitionSpec as P

F0 = 8


def tables(count_t, count_f, first):
    times = jnp.arange(count_t, dtype=jnp.int32)
    freqs = first + jnp.arange(count_f, dtype=jnp.int32)
    phase = freqs[:, None] * times[None, :] % count_t
    angle = phase.astype(jnp.float32) * (2.0 * math.pi / count_t)
    rows = jnp.stack([jnp.cos(angle), -jnp.sin(angle)], 1).reshape(2 * count_f, count_t)
    forward = (rows / math.sqrt(count_t)).astype(jnp.bfloat16)
    inverse = (rows / math.sqrt(count_f)).astype(jnp.bfloat16)
    return (forward, inverse)


def combine(mirror_real, mirror_imag, sq_real, sq_imag, cube_real, cube_imag, wave_real, wave_imag):
    two_real = wave_real * wave_real - wave_imag * wave_imag
    two_imag = 2.0 * wave_real * wave_imag
    out_real = (
        mirror_real
        - (wave_real * sq_real - wave_imag * sq_imag)
        + (two_real * cube_real - two_imag * cube_imag)
    )
    out_imag = (
        mirror_imag
        - (wave_real * sq_imag + wave_imag * sq_real)
        + (two_real * cube_imag + two_imag * cube_real)
    )
    return (out_real, out_imag)


def multiply(left_side, right_side):
    return jnp.einsum("fmk,fkn->fmn", left_side, right_side, preferred_element_type=jnp.float32)


def complex_product(left_side, right_side):
    real_part = multiply(left_side[:, 0], right_side[:, 0]) - multiply(
        left_side[:, 1], right_side[:, 1]
    )
    imag_part = multiply(left_side[:, 0], right_side[:, 1]) + multiply(
        left_side[:, 1], right_side[:, 0]
    )
    return (real_part, imag_part)


def local_sliced(wavefield, inverse_wavelet):
    src_rows, rcv_cols, samples = wavefield.shape
    count_f = inverse_wavelet.shape[1]
    groups = lax.axis_size("rcv")
    per_dev = count_f // groups
    forward, inverse = tables(samples, count_f, F0)
    spectra = jnp.einsum(
        "ct,srt->csr", forward, wavefield, preferred_element_type=jnp.float32
    ).astype(jnp.bfloat16)
    spectra = spectra.reshape(groups, 2 * per_dev, src_rows, rcv_cols)
    slices = lax.all_to_all(spectra, "rcv", split_axis=0, concat_axis=3, tiled=True)
    total_cols = slices.shape[3]
    slices = slices.reshape(per_dev, 2, src_rows, total_cols)
    whole = lax.all_gather(slices, "src", axis=2, tiled=True).astype(jnp.float32)
    all_rows = (0.5 * (whole + jnp.swapaxes(whole, 2, 3))).astype(jnp.bfloat16)
    mirrored = lax.dynamic_slice_in_dim(all_rows, lax.axis_index("src") * src_rows, src_rows, 2)
    sq_real, sq_imag = complex_product(mirrored, all_rows)
    squared = jnp.stack([sq_real, sq_imag], 1).astype(jnp.bfloat16)
    cube_real, cube_imag = complex_product(squared, all_rows)
    wavelet = lax.dynamic_slice_in_dim(inverse_wavelet, lax.axis_index("rcv") * per_dev, per_dev, 1)
    wave_real = wavelet[0][:, None, None]
    wave_imag = wavelet[1][:, None, None]
    out_real, out_imag = combine(
        mirrored[:, 0].astype(jnp.float32),
        mirrored[:, 1].astype(jnp.float32),
        sq_real,
        sq_imag,
        cube_real,
        cube_imag,
        wave_real,
        wave_imag,
    )
    cleaned = (
        jnp.stack([out_real, out_imag], 1)
        .astype(jnp.bfloat16)
        .reshape(1, 2 * per_dev, src_rows, total_cols)
    )
    returned = lax.all_to_all(cleaned, "rcv", split_axis=3, concat_axis=0, tiled=True)
    returned = returned.reshape(2 * count_f, src_rows, rcv_cols)
    return jnp.einsum("csr,ct->srt", returned, inverse, preferred_element_type=jnp.float32).astype(
        jnp.bfloat16
    )


NT_DIMS = (((1,), (1,)), ((), ()))
TN_DIMS = (((0,), (0,)), ((), ()))
EDGE = 32


def dft_kernel(table_ref, wave_ref, out_ref, *, group):
    rows, cols, samples = wave_ref.shape
    for first in range(0, rows, group):
        flat = wave_ref[first : first + group].reshape(group * cols, samples)
        values = lax.dot_general(flat, table_ref[...], NT_DIMS, preferred_element_type=jnp.float32)
        turned = [values[row * cols : (row + 1) * cols].T for row in range(group)]
        stacked = jnp.swapaxes(jnp.stack(turned, 0), 0, 1)
        out_ref[:, first : first + group, :] = stacked.astype(out_ref.dtype)


def dft(table, wave, start, count, step):
    _, cols, samples = wave.shape
    bins = table.shape[0]
    skip = start // step
    return pl.pallas_call(
        functools.partial(dft_kernel, group=16),
        grid=(count // step,),
        in_specs=[
            pl.BlockSpec((bins, samples), lambda i: (0, 0)),
            pl.BlockSpec((step, cols, samples), lambda i: (i + skip, 0, 0)),
        ],
        out_specs=pl.BlockSpec((bins, step, cols), lambda i: (0, i, 0)),
        out_shape=jax.ShapeDtypeStruct((bins, count, cols), jnp.bfloat16),
        cost_estimate=pl.CostEstimate(
            flops=2 * bins * samples * count * cols,
            bytes_accessed=2 * count * cols * (samples + bins),
            transcendentals=0,
        ),
        compiler_params=pltpu.CompilerParams(vmem_limit_bytes=56 << 20),
        name="forward_table",
    )(table, wave)


def inverse_kernel(table_ref, first_ref, last_ref, *refs):
    out_ref = refs[-1]
    table = table_ref[...]
    both = jnp.swapaxes(jnp.concatenate([first_ref[...], last_ref[...]], 0), 0, 1)
    for row in range(out_ref.shape[0]):
        out_ref[row] = lax.dot_general(
            both[row], table, TN_DIMS, preferred_element_type=jnp.float32
        ).astype(out_ref.dtype)


def inverse_rows(table, first, last, start, step, prior=None):
    bins, samples = table.shape
    half, total, cols = first.shape
    count = last.shape[1]
    skip = start // step
    return pl.pallas_call(
        inverse_kernel,
        grid=(count // step,),
        in_specs=[
            pl.BlockSpec((bins, samples), lambda i: (0, 0)),
            pl.BlockSpec((half, step, cols), lambda i: (0, i + skip, 0)),
            pl.BlockSpec((bins - half, step, cols), lambda i: (0, i, 0)),
        ]
        + ([] if prior is None else [pl.BlockSpec(memory_space=pl.ANY)]),
        out_specs=pl.BlockSpec((step, cols, samples), lambda i: (i + skip, 0, 0)),
        out_shape=jax.ShapeDtypeStruct((total, cols, samples), jnp.bfloat16),
        input_output_aliases={} if prior is None else {3: 0},
        cost_estimate=pl.CostEstimate(
            flops=2 * bins * samples * count * cols,
            bytes_accessed=2 * count * cols * (samples + bins),
            transcendentals=0,
        ),
        compiler_params=pltpu.CompilerParams(vmem_limit_bytes=56 << 20),
        name="inverse_table",
    )(table, first, last, *([] if prior is None else [prior]))


def tri(value, other, upper):
    row = lax.broadcasted_iota(jnp.int32, value.shape, 0)
    col = lax.broadcasted_iota(jnp.int32, value.shape, 1)
    return jnp.where(row <= col, value, other) if upper else jnp.where(row > col, value, other)


def diagonal(value):
    row = lax.broadcasted_iota(jnp.int32, value.shape, 0)
    col = lax.broadcasted_iota(jnp.int32, value.shape, 1)
    return jnp.sum(jnp.where(row == col, value, 0.0), axis=0, keepdims=True)


def with_diagonal(value, line):
    row = lax.broadcasted_iota(jnp.int32, value.shape, 0)
    col = lax.broadcasted_iota(jnp.int32, value.shape, 1)
    return jnp.where(row == col, jnp.broadcast_to(line, value.shape), value)


EXTRA = 8


def fold_kernel(place_ref, whole_ref, swap_ref, two_ref, three_ref, last_ref, out_ref):
    count, length, cols = whole_ref.shape
    kept = out_ref.shape[1] - EXTRA
    turn, side, lower = place_ref[0], place_ref[1], place_ref[2]

    def plane(d, part, half):
        start = (2 * part + half) * cols
        return whole_ref[d, start : start + cols]

    def each(d, carry):
        @pl.when(turn == 0)
        def _():
            for half in range(2):
                real = plane(d, 0, half).astype(jnp.float32)
                imag = plane(d, 1, half).astype(jnp.float32)
                span = slice(half * cols, (half + 1) * cols)

                @pl.when(side == half)
                def _():
                    mean_real = 0.5 * (real + real.T)
                    mean_imag = 0.5 * (imag + imag.T)
                    out_ref[d, span] = tri(mean_real, mean_imag, True).astype(out_ref.dtype)
                    line = jnp.broadcast_to(diagonal(mean_imag), (EXTRA, cols))
                    out_ref[d, kept:] = line.astype(out_ref.dtype)

                @pl.when(side != half)
                def _():
                    own = imag if half else real
                    mean = 0.5 * (own + swap_ref[d].astype(jnp.float32).T)
                    out_ref[d, span] = mean.astype(out_ref.dtype)

            middle = 2 * cols + two_ref.shape[1]
            out_ref[d, 2 * cols : middle] = two_ref[d]
            out_ref[d, middle:kept] = three_ref[d]

        @pl.when(turn == 1)
        def _():
            for half in range(2):

                @pl.when(side == half)
                def _():
                    own = jnp.where(lower == 1, plane(d, 0, half), plane(d, 1, half))
                    mean = 0.5 * (own.astype(jnp.float32) + swap_ref[d].astype(jnp.float32).T)
                    out_ref[d, :cols] = mean.astype(out_ref.dtype)

                @pl.when(side != half)
                def _():
                    out_ref[d, cols : 2 * cols] = plane(d, 0, half)
                    out_ref[d, 2 * cols : 3 * cols] = plane(d, 1, half)

            out_ref[d, 3 * cols : kept] = last_ref[d]
            out_ref[d, kept:] = jnp.zeros((EXTRA, cols), out_ref.dtype)

        @pl.when(turn > 1)
        def _():
            out_ref[d, :kept] = whole_ref[d, :kept]
            out_ref[d, kept:] = jnp.zeros((EXTRA, cols), out_ref.dtype)

        return carry

    lax.fori_loop(0, count, each, 0)


def unfold_kernel(place_ref, folded_ref, swap_ref, two_ref, three_ref, last_ref, out_ref):
    count, length, cols = out_ref.shape
    kept = folded_ref.shape[1] - EXTRA
    turn, side, lower = place_ref[0], place_ref[1], place_ref[2]

    def each(d, carry):
        @pl.when(turn == 0)
        def _():
            for half in range(2):
                own = folded_ref[d, half * cols : (half + 1) * cols]
                real = slice(half * cols, (half + 1) * cols)
                imag = slice((2 + half) * cols, (3 + half) * cols)

                @pl.when(side == half)
                def _():
                    packed = own.astype(jnp.float32)
                    line = folded_ref[d, kept:].astype(jnp.float32)[:1]
                    out_ref[d, real] = tri(packed, packed.T, True).astype(out_ref.dtype)
                    below = with_diagonal(tri(packed, packed.T, False), line)
                    out_ref[d, imag] = below.astype(out_ref.dtype)

                @pl.when(side != half)
                def _():
                    other = swap_ref[d].astype(jnp.float32).T.astype(out_ref.dtype)
                    out_ref[d, imag if half else real] = own
                    out_ref[d, real if half else imag] = other

        @pl.when(turn == 1)
        def _():
            for half in range(2):
                real = slice(half * cols, (half + 1) * cols)
                imag = slice((2 + half) * cols, (3 + half) * cols)

                @pl.when(side == half)
                def _():
                    own = folded_ref[d, :cols]
                    other = swap_ref[d].astype(jnp.float32).T.astype(out_ref.dtype)
                    out_ref[d, real] = jnp.where(lower == 1, own, other)
                    out_ref[d, imag] = jnp.where(lower == 1, other, own)

                @pl.when(side != half)
                def _():
                    out_ref[d, real] = folded_ref[d, cols : 2 * cols]
                    out_ref[d, imag] = folded_ref[d, 2 * cols : 3 * cols]

        @pl.when(turn > 1)
        def _():
            out_ref[d, :kept] = folded_ref[d, :kept]

        @pl.when(turn == 2)
        def _():
            out_ref[d, kept:] = two_ref[d]

        @pl.when(turn == 3)
        def _():
            middle = kept + three_ref.shape[1]
            out_ref[d, kept:middle] = three_ref[d]
            out_ref[d, middle:] = last_ref[d]

        return carry

    lax.fori_loop(0, count, each, 0)


def per_device(kernel, place, first, swap, hands, shape, name, step=8):
    devices = first.shape[0]

    def spec(array_shape):
        rest = len(array_shape) - 1
        return pl.BlockSpec((step,) + tuple(array_shape[1:]), lambda i: (i,) + (0,) * rest)

    return pl.pallas_call(
        kernel,
        grid=(devices // step,),
        in_specs=[pl.BlockSpec(memory_space=pltpu.SMEM)]
        + [spec(a.shape) for a in (first, swap, *hands)],
        out_specs=spec(shape),
        out_shape=jax.ShapeDtypeStruct(shape, first.dtype),
        cost_estimate=pl.CostEstimate(
            flops=4 * first.size, bytes_accessed=8 * first.size, transcendentals=0
        ),
        name=name,
    )(place, first, swap, *hands)


def owner_kernel(wave_ref, recv_ref, *refs, sources, groups, cols, fold_in, fold_out):
    out_refs, (held, done) = refs[:-2], refs[-2:]
    out_ref = out_refs[0]
    halves = groups // sources
    rows = halves * cols
    quarter = cols // 4
    kept = 3 * cols + quarter

    def at(block):
        return pl.ds(pl.multiple_of(block * cols, cols), cols)

    def load(d, start):
        return recv_ref[d, start * cols : (start + 1) * cols].astype(jnp.float32)

    def moved(src, col, turn):
        two, three = 2 * cols, 2 * cols + 3 * quarter
        if turn == 2:
            return [(src * groups + col, two, three)]
        return [
            (src * groups + col, three, kept),
            ((src ^ 1) * groups + col, 3 * cols, kept),
        ]

    def load_kept(part, half, src, col, owner_src, turn):
        if part == 0 or half == 0:
            return load(src * groups + col, part * halves + half)
        spans = [(src * groups + col, 3 * cols, kept)] + moved(owner_src, col, turn)
        return jnp.concatenate(
            [recv_ref[d, start:stop].astype(jnp.float32) for d, start, stop in spans], 0
        )

    def put(part, row, col, value):
        held[part, at(row), at(col)] = value.astype(jnp.bfloat16)

    def mirror_whole(src, carry):
        for half in range(halves):
            block = src * halves + half
            for part in range(2):
                for col in range(groups):
                    a = load(src * groups + col, part * halves + half)
                    b = load((col // halves) * groups + block, part * halves + col % halves)
                    put(part, block, col, 0.5 * (a + b.T))
        return carry

    def mirror_folded(src, carry):
        for turn in range(2, sources):
            other = src ^ turn
            for half in range(halves):
                row = src * halves + half
                for side in range(halves):
                    col = other * halves + side
                    for part in range(2):
                        a = load_kept(part, half, src, col, other, turn)
                        b = load_kept(part, side, other, row, src, turn)
                        put(part, row, col, 0.5 * (a + b.T))
        low, high = src * halves, src * halves + 1
        for side in range(halves):
            block = src * halves + side
            d = src * groups + block
            packed = load(d, side)
            line = recv_ref[d, kept:].astype(jnp.float32)[:1]
            put(0, block, block, tri(packed, packed.T, True))
            put(1, block, block, with_diagonal(tri(packed, packed.T, False), line))
        real = load(src * groups + high, 0)
        imag = load(src * groups + low, 1)
        put(0, low, high, real)
        put(0, high, low, real.T)
        put(1, high, low, imag)
        put(1, low, high, imag.T)
        return carry

    def mirror_near(pair, carry):
        low, high = 2 * pair, 2 * pair + 1
        for half in range(halves):
            row, col = low * halves + half, high * halves + half
            real = load(low * groups + col, 0)
            imag = load(high * groups + row, 0)
            put(0, row, col, real)
            put(0, col, row, real.T)
            put(1, col, row, imag)
            put(1, row, col, imag.T)
            col = high * halves + 1 - half
            for part in range(2):
                a = load(low * groups + col, 1 + part)
                b = load(high * groups + row, 1 + part)
                mean = 0.5 * (a + b.T)
                put(part, row, col, mean)
                put(part, col, row, mean.T)
        return carry

    if fold_in:
        lax.fori_loop(0, sources, mirror_folded, 0)
        lax.fori_loop(0, sources // 2, mirror_near, 0)
    else:
        lax.fori_loop(0, sources, mirror_whole, 0)

    wave_real, wave_imag = wave_ref[0], wave_ref[1]
    two_real = wave_real * wave_real - wave_imag * wave_imag
    two_imag = 2.0 * wave_real * wave_imag

    def dot(left, right):
        return jnp.dot(left, right, preferred_element_type=jnp.float32)

    def product(src, carry):
        span = pl.ds(pl.multiple_of(src * rows, rows), rows)
        real, imag = held[0, span, :], held[1, span, :]
        sq_real = dot(real, held[0]) - dot(imag, held[1])
        sq_imag = dot(real, held[1]) + dot(imag, held[0])
        out_real = real.astype(jnp.float32) - (wave_real * sq_real - wave_imag * sq_imag)
        out_imag = imag.astype(jnp.float32) - (wave_real * sq_imag + wave_imag * sq_real)
        left_real, left_imag = sq_real.astype(jnp.bfloat16), sq_imag.astype(jnp.bfloat16)
        cube_real = dot(left_real, held[0]) - dot(left_imag, held[1])
        cube_imag = dot(left_real, held[1]) + dot(left_imag, held[0])
        out_real = (out_real + (two_real * cube_real - two_imag * cube_imag)).astype(jnp.bfloat16)
        out_imag = (out_imag + (two_real * cube_imag + two_imag * cube_real)).astype(jnp.bfloat16)
        if fold_out:
            done[0, span, :] = out_real
            done[1, span, :] = out_imag
        else:
            top = out_refs[0].shape[1] // 2
            for col in range(groups):
                for part, value in enumerate((out_real, out_imag)):
                    tile = value[:, col * cols : (col + 1) * cols]
                    d = src * groups + col
                    out_refs[0][d, part * top : (part + 1) * top] = tile[:top]
                    out_refs[1][d, part * (rows - top) : (part + 1) * (rows - top)] = tile[top:]
        return carry

    lax.fori_loop(0, sources, product, 0)
    if not fold_out:
        return

    def pack(src, carry):
        span = pl.ds(pl.multiple_of(src * rows, rows), rows)
        for turn in range(2, sources):
            other = src ^ turn
            for side in range(halves):
                col = other * halves + side
                d = src * groups + col
                imag = done[1, span, at(col)]
                out_ref[d, :rows] = done[0, span, at(col)]
                out_ref[d, rows:kept] = imag[: kept - rows]
                out_ref[d, kept:] = jnp.zeros((EXTRA, cols), jnp.bfloat16)
                first = kept - rows
                for place, start, stop in moved(other, col, turn):
                    out_ref[place, start:stop] = imag[first : first + stop - start]
                    first += stop - start
        for side in range(halves):
            block = src * halves + side
            d = src * groups + block
            real = done[0, at(block), at(block)].astype(jnp.float32)
            imag = done[1, at(block), at(block)].astype(jnp.float32)
            out_ref[d, side * cols : (side + 1) * cols] = tri(real, imag, True).astype(jnp.bfloat16)
            line = jnp.broadcast_to(diagonal(imag), (EXTRA, cols))
            out_ref[d, kept:] = line.astype(jnp.bfloat16)
        low, high = src * halves, src * halves + 1
        out_ref[src * groups + high, :cols] = done[0, at(low), at(high)]
        out_ref[src * groups + low, cols : 2 * cols] = done[1, at(high), at(low)]
        return carry

    def pack_near(pair, carry):
        low, high = 2 * pair, 2 * pair + 1
        for half in range(halves):
            row, col = low * halves + half, high * halves + half
            out_ref[low * groups + col, :cols] = done[0, at(row), at(col)]
            out_ref[high * groups + row, :cols] = done[1, at(col), at(row)]
            col = high * halves + 1 - half
            for part in range(2):
                slot = slice((1 + part) * cols, (2 + part) * cols)
                out_ref[low * groups + col, slot] = done[part, at(row), at(col)]
                out_ref[high * groups + row, slot] = done[part, at(col), at(row)]
            for d in (low * groups + col, high * groups + row):
                out_ref[d, kept:] = jnp.zeros((EXTRA, cols), jnp.bfloat16)
        return carry

    lax.fori_loop(0, sources, pack, 0)
    lax.fori_loop(0, sources // 2, pack_near, 0)


def owner(wave, recv, sources, groups, fold_in, fold_out):
    devices, _, cols = recv.shape
    total = groups * cols
    whole = 2 * (total // sources)
    lengths = [3 * cols + cols // 4 + EXTRA] if fold_out else [whole - 2 * EDGE, 2 * EDGE]
    return pl.pallas_call(
        functools.partial(
            owner_kernel,
            sources=sources,
            groups=groups,
            cols=cols,
            fold_in=fold_in,
            fold_out=fold_out,
        ),
        in_specs=[
            pl.BlockSpec(memory_space=pltpu.SMEM),
            pl.BlockSpec(memory_space=pltpu.VMEM),
        ],
        out_specs=[pl.BlockSpec(memory_space=pltpu.VMEM)] * len(lengths),
        out_shape=[jax.ShapeDtypeStruct((devices, n, cols), recv.dtype) for n in lengths],
        scratch_shapes=[
            pltpu.VMEM((2, total, total), jnp.bfloat16),
            pltpu.VMEM((2, total, total) if fold_out else (2, 16, 128), jnp.bfloat16),
        ],
        cost_estimate=pl.CostEstimate(
            flops=16 * total**3,
            bytes_accessed=8 * devices * whole * cols,
            transcendentals=0,
        ),
        compiler_params=pltpu.CompilerParams(vmem_limit_bytes=56 << 20),
        name="owned_frequency",
    )(wave, recv)


AXES = ("src", "rcv")


def swap_pairs(sources, groups):
    halves = groups // sources
    pairs = []
    for src in range(sources):
        for side in range(halves):
            here = src * groups + src * halves + side
            pairs.append((here, src * groups + src * halves + 1 - side))
            near = src ^ 1
            pairs.append(
                (near * groups + src * halves + side, src * groups + near * halves + side)
            )
    return pairs


def turn_pairs(sources, groups, start, stop):
    halves = groups // sources
    return [
        ((col // halves ^ start) * groups + col, (col // halves ^ stop) * groups + col)
        for col in range(groups)
    ]


def where_am_i(sources, groups):
    halves = groups // sources
    src, col = lax.axis_index("src"), lax.axis_index("rcv")
    turn, side = src ^ (col // halves), col % halves
    place = jnp.stack([turn, side, (src < col // halves).astype(jnp.int32)])
    return turn, side, place.astype(jnp.int32)


def send_rows(array, start, stop, pairs):
    return lax.ppermute(array[:, start:stop], AXES, pairs)


def fold(spectra, sources, groups):
    devices, length, cols = spectra.shape
    quarter = cols // 4
    kept = 3 * cols + quarter
    turn, side, place = where_am_i(sources, groups)
    diagonal_plane = jnp.where(side == 0, 1, 2)
    near_plane = jnp.where(place[2] == 1, 2 + side, side)
    plane = jnp.where(turn == 0, diagonal_plane, near_plane)
    block = lax.dynamic_slice_in_dim(spectra, plane * cols, cols, 1)
    swap = lax.ppermute(block, AXES, swap_pairs(sources, groups))
    hands = [
        send_rows(spectra, kept, length, turn_pairs(sources, groups, 2, 0)),
        send_rows(spectra, kept, kept + 2 * quarter, turn_pairs(sources, groups, 3, 0)),
        send_rows(spectra, kept + 2 * quarter, length, turn_pairs(sources, groups, 3, 1)),
    ]
    shape = (devices, kept + EXTRA, cols)
    return per_device(fold_kernel, place, spectra, swap, hands, shape, "fold")


def unfold(folded, sources, groups):
    devices, length, cols = folded.shape
    quarter = cols // 4
    kept = 3 * cols + quarter
    middle = 2 * cols + 3 * quarter
    turn, side, place = where_am_i(sources, groups)
    plane = jnp.where(turn == 0, 1 - side, 0)
    block = lax.dynamic_slice_in_dim(folded, plane * cols, cols, 1)
    swap = lax.ppermute(block, AXES, swap_pairs(sources, groups))
    hands = [
        send_rows(folded, 2 * cols, middle, turn_pairs(sources, groups, 0, 2)),
        send_rows(folded, middle, kept, turn_pairs(sources, groups, 0, 3)),
        send_rows(folded, 3 * cols, kept, turn_pairs(sources, groups, 1, 3)),
    ]
    shape = (devices, 4 * cols, cols)
    return per_device(unfold_kernel, place, folded, swap, hands, shape, "unfold")


def exchange(array):
    return lax.all_to_all(array, AXES, 0, 0, tiled=True)


def local_whole(wavefield, inverse_wavelet):
    src_rows, rcv_cols, samples = wavefield.shape
    count_f = inverse_wavelet.shape[1]
    sources, groups = lax.axis_size("src"), lax.axis_size("rcv")
    devices = sources * groups
    me = lax.axis_index(AXES)
    forward, inverse = tables(samples, count_f, F0)
    width = 2 * devices
    wavelets = [
        lax.dynamic_index_in_dim(inverse_wavelet, start + me, 1, keepdims=False)
        for start in range(0, count_f, devices)
    ]

    def spectra(chunk, start, count, step):
        rows = dft(forward[chunk * width : (chunk + 1) * width], wavefield, start, count, step)
        return rows.reshape(devices, 2 * count, rcv_cols)

    plain = exchange(spectra(0, 0, src_rows, src_rows // 2))
    folded = exchange(fold(spectra(1, 0, src_rows, src_rows // 2), sources, groups))
    (cleaned,) = owner(wavelets[0], plain, sources, groups, False, True)
    first = unfold(exchange(cleaned), sources, groups).reshape(width, src_rows, rcv_cols)
    most, rest = owner(wavelets[1], folded, sources, groups, True, False)
    most, rest, first = lax.optimization_barrier((exchange(most), rest, first))
    rest = exchange(rest)
    most = most.reshape(width, src_rows - EDGE, rcv_cols)
    rest = rest.reshape(width, EDGE, rcv_cols)
    out = inverse_rows(inverse, first, most, 0, (src_rows - EDGE) // 2)
    return inverse_rows(inverse, first, rest, src_rows - EDGE, EDGE, out)


def solution(mesh):
    placed = (P("src", "rcv", None), P())

    def local(wavefield, inverse_wavelet):
        sources, groups = lax.axis_size("src"), lax.axis_size("rcv")
        fits = inverse_wavelet.shape[1] == 2 * sources * groups
        if fits and sources == 4 and groups == 2 * sources:
            return local_whole(wavefield, inverse_wavelet)
        return local_sliced(wavefield, inverse_wavelet)

    return jax.shard_map(
        local, mesh=mesh, in_specs=placed, out_specs=P("src", "rcv", None), check_vma=False
    )
```

```python
import functools
import math

import jax
import jax.numpy as jnp
from jax import lax
from jax.experimental import pallas as pl
from jax.experimental.pallas import tpu as pltpu
from jax.sharding import PartitionSpec as P

F0 = 8


def tables(count_t, count_f, first):
    times = jnp.arange(count_t, dtype=jnp.int32)
    freqs = first + jnp.arange(count_f, dtype=jnp.int32)
    phase = freqs[:, None] * times[None, :] % count_t
    angle = phase.astype(jnp.float32) * (2.0 * math.pi / count_t)
    rows = jnp.stack([jnp.cos(angle), -jnp.sin(angle)], 1).reshape(2 * count_f, count_t)
    forward = (rows / math.sqrt(count_t)).astype(jnp.bfloat16)
    inverse = (rows / math.sqrt(count_f)).astype(jnp.bfloat16)
    return (forward, inverse)


def combine(mirror_real, mirror_imag, sq_real, sq_imag, cube_real, cube_imag, wave_real, wave_imag):
    two_real = wave_real * wave_real - wave_imag * wave_imag
    two_imag = 2.0 * wave_real * wave_imag
    out_real = (
        mirror_real
        - (wave_real * sq_real - wave_imag * sq_imag)
        + (two_real * cube_real - two_imag * cube_imag)
    )
    out_imag = (
        mirror_imag
        - (wave_real * sq_imag + wave_imag * sq_real)
        + (two_real * cube_imag + two_imag * cube_real)
    )
    return (out_real, out_imag)


def multiply(left_side, right_side):
    return jnp.einsum("fmk,fkn->fmn", left_side, right_side, preferred_element_type=jnp.float32)


def complex_product(left_side, right_side):
    real_part = multiply(left_side[:, 0], right_side[:, 0]) - multiply(
        left_side[:, 1], right_side[:, 1]
    )
    imag_part = multiply(left_side[:, 0], right_side[:, 1]) + multiply(
        left_side[:, 1], right_side[:, 0]
    )
    return (real_part, imag_part)


def local_sliced(wavefield, inverse_wavelet):
    src_rows, rcv_cols, samples = wavefield.shape
    count_f = inverse_wavelet.shape[1]
    groups = lax.axis_size("rcv")
    per_dev = count_f // groups
    forward, inverse = tables(samples, count_f, F0)
    spectra = jnp.einsum(
        "ct,srt->csr", forward, wavefield, preferred_element_type=jnp.float32
    ).astype(jnp.bfloat16)
    spectra = spectra.reshape(groups, 2 * per_dev, src_rows, rcv_cols)
    slices = lax.all_to_all(spectra, "rcv", split_axis=0, concat_axis=3, tiled=True)
    total_cols = slices.shape[3]
    slices = slices.reshape(per_dev, 2, src_rows, total_cols)
    whole = lax.all_gather(slices, "src", axis=2, tiled=True).astype(jnp.float32)
    all_rows = (0.5 * (whole + jnp.swapaxes(whole, 2, 3))).astype(jnp.bfloat16)
    mirrored = lax.dynamic_slice_in_dim(all_rows, lax.axis_index("src") * src_rows, src_rows, 2)
    sq_real, sq_imag = complex_product(mirrored, all_rows)
    squared = jnp.stack([sq_real, sq_imag], 1).astype(jnp.bfloat16)
    cube_real, cube_imag = complex_product(squared, all_rows)
    wavelet = lax.dynamic_slice_in_dim(inverse_wavelet, lax.axis_index("rcv") * per_dev, per_dev, 1)
    wave_real = wavelet[0][:, None, None]
    wave_imag = wavelet[1][:, None, None]
    out_real, out_imag = combine(
        mirrored[:, 0].astype(jnp.float32),
        mirrored[:, 1].astype(jnp.float32),
        sq_real,
        sq_imag,
        cube_real,
        cube_imag,
        wave_real,
        wave_imag,
    )
    cleaned = (
        jnp.stack([out_real, out_imag], 1)
        .astype(jnp.bfloat16)
        .reshape(1, 2 * per_dev, src_rows, total_cols)
    )
    returned = lax.all_to_all(cleaned, "rcv", split_axis=3, concat_axis=0, tiled=True)
    returned = returned.reshape(2 * count_f, src_rows, rcv_cols)
    return jnp.einsum("csr,ct->srt", returned, inverse, preferred_element_type=jnp.float32).astype(
        jnp.bfloat16
    )


NT_DIMS = (((1,), (1,)), ((), ()))
TN_DIMS = (((0,), (0,)), ((), ()))
EDGE = 32


def dft_kernel(table_ref, wave_ref, out_ref, *, group):
    rows, cols, samples = wave_ref.shape
    for first in range(0, rows, group):
        flat = wave_ref[first : first + group].reshape(group * cols, samples)
        values = lax.dot_general(flat, table_ref[...], NT_DIMS, preferred_element_type=jnp.float32)
        turned = [values[row * cols : (row + 1) * cols].T for row in range(group)]
        stacked = jnp.swapaxes(jnp.stack(turned, 0), 0, 1)
        out_ref[:, first : first + group, :] = stacked.astype(out_ref.dtype)


def dft(table, wave, start, count, step):
    _, cols, samples = wave.shape
    bins = table.shape[0]
    skip = start // step
    return pl.pallas_call(
        functools.partial(dft_kernel, group=16),
        grid=(count // step,),
        in_specs=[
            pl.BlockSpec((bins, samples), lambda i: (0, 0)),
            pl.BlockSpec((step, cols, samples), lambda i: (i + skip, 0, 0)),
        ],
        out_specs=pl.BlockSpec((bins, step, cols), lambda i: (0, i, 0)),
        out_shape=jax.ShapeDtypeStruct((bins, count, cols), jnp.bfloat16),
        cost_estimate=pl.CostEstimate(
            flops=2 * bins * samples * count * cols,
            bytes_accessed=2 * count * cols * (samples + bins),
            transcendentals=0,
        ),
        compiler_params=pltpu.CompilerParams(vmem_limit_bytes=56 << 20),
        name="forward_table",
    )(table, wave)


def inverse_kernel(table_ref, first_ref, last_ref, *refs):
    out_ref = refs[-1]
    table = table_ref[...]
    both = jnp.swapaxes(jnp.concatenate([first_ref[...], last_ref[...]], 0), 0, 1)
    for row in range(out_ref.shape[0]):
        out_ref[row] = lax.dot_general(
            both[row], table, TN_DIMS, preferred_element_type=jnp.float32
        ).astype(out_ref.dtype)


def inverse_rows(table, first, last, start, step, prior=None):
    bins, samples = table.shape
    half, total, cols = first.shape
    count = last.shape[1]
    last_spec = pl.BlockSpec((bins - half, step, cols), lambda i: (0, i, 0))
    if count == step:
        last = pltpu.with_memory_space_constraint(last, pltpu.VMEM)
        last_spec = pl.BlockSpec(memory_space=pltpu.VMEM)
    skip = start // step
    return pl.pallas_call(
        inverse_kernel,
        grid=(count // step,),
        in_specs=[
            pl.BlockSpec((bins, samples), lambda i: (0, 0)),
            pl.BlockSpec((half, step, cols), lambda i: (0, i + skip, 0)),
            last_spec,
        ]
        + ([] if prior is None else [pl.BlockSpec(memory_space=pl.ANY)]),
        out_specs=pl.BlockSpec((step, cols, samples), lambda i: (i + skip, 0, 0)),
        out_shape=jax.ShapeDtypeStruct((total, cols, samples), jnp.bfloat16),
        input_output_aliases={} if prior is None else {3: 0},
        cost_estimate=pl.CostEstimate(
            flops=2 * bins * samples * count * cols,
            bytes_accessed=2 * count * cols * (samples + bins),
            transcendentals=0,
        ),
        compiler_params=pltpu.CompilerParams(vmem_limit_bytes=56 << 20),
        name="inverse_table",
    )(table, first, last, *([] if prior is None else [prior]))


def tri(value, other, upper):
    row = lax.broadcasted_iota(jnp.int32, value.shape, 0)
    col = lax.broadcasted_iota(jnp.int32, value.shape, 1)
    return jnp.where(row <= col, value, other) if upper else jnp.where(row > col, value, other)


def diagonal(value):
    row = lax.broadcasted_iota(jnp.int32, value.shape, 0)
    col = lax.broadcasted_iota(jnp.int32, value.shape, 1)
    return jnp.sum(jnp.where(row == col, value, 0.0), axis=0, keepdims=True)


def with_diagonal(value, line):
    row = lax.broadcasted_iota(jnp.int32, value.shape, 0)
    col = lax.broadcasted_iota(jnp.int32, value.shape, 1)
    return jnp.where(row == col, jnp.broadcast_to(line, value.shape), value)


EXTRA = 8


def fold_kernel(place_ref, whole_ref, swap_ref, two_ref, three_ref, last_ref, out_ref):
    count, length, cols = whole_ref.shape
    kept = out_ref.shape[1] - EXTRA
    turn, side, lower = place_ref[0], place_ref[1], place_ref[2]

    def plane(d, part, half):
        start = (2 * part + half) * cols
        return whole_ref[d, start : start + cols]

    def each(d, carry):
        @pl.when(turn == 0)
        def _():
            for half in range(2):
                real = plane(d, 0, half).astype(jnp.float32)
                imag = plane(d, 1, half).astype(jnp.float32)
                span = slice(half * cols, (half + 1) * cols)

                @pl.when(side == half)
                def _():
                    mean_real = 0.5 * (real + real.T)
                    mean_imag = 0.5 * (imag + imag.T)
                    out_ref[d, span] = tri(mean_real, mean_imag, True).astype(out_ref.dtype)
                    line = jnp.broadcast_to(diagonal(mean_imag), (EXTRA, cols))
                    out_ref[d, kept:] = line.astype(out_ref.dtype)

                @pl.when(side != half)
                def _():
                    own = imag if half else real
                    mean = 0.5 * (own + swap_ref[d].astype(jnp.float32).T)
                    out_ref[d, span] = mean.astype(out_ref.dtype)

            middle = 2 * cols + two_ref.shape[1]
            out_ref[d, 2 * cols : middle] = two_ref[d]
            out_ref[d, middle:kept] = three_ref[d]

        @pl.when(turn == 1)
        def _():
            for half in range(2):

                @pl.when(side == half)
                def _():
                    own = jnp.where(lower == 1, plane(d, 0, half), plane(d, 1, half))
                    mean = 0.5 * (own.astype(jnp.float32) + swap_ref[d].astype(jnp.float32).T)
                    out_ref[d, :cols] = mean.astype(out_ref.dtype)

                @pl.when(side != half)
                def _():
                    out_ref[d, cols : 2 * cols] = plane(d, 0, half)
                    out_ref[d, 2 * cols : 3 * cols] = plane(d, 1, half)

            out_ref[d, 3 * cols : kept] = last_ref[d]
            out_ref[d, kept:] = jnp.zeros((EXTRA, cols), out_ref.dtype)

        @pl.when(turn > 1)
        def _():
            out_ref[d, :kept] = whole_ref[d, :kept]
            out_ref[d, kept:] = jnp.zeros((EXTRA, cols), out_ref.dtype)

        return carry

    lax.fori_loop(0, count, each, 0)


def unfold_kernel(place_ref, folded_ref, swap_ref, two_ref, three_ref, last_ref, out_ref):
    count, length, cols = out_ref.shape
    kept = folded_ref.shape[1] - EXTRA
    turn, side, lower = place_ref[0], place_ref[1], place_ref[2]

    def each(d, carry):
        @pl.when(turn == 0)
        def _():
            for half in range(2):
                own = folded_ref[d, half * cols : (half + 1) * cols]
                real = slice(half * cols, (half + 1) * cols)
                imag = slice((2 + half) * cols, (3 + half) * cols)

                @pl.when(side == half)
                def _():
                    packed = own.astype(jnp.float32)
                    line = folded_ref[d, kept:].astype(jnp.float32)[:1]
                    out_ref[d, real] = tri(packed, packed.T, True).astype(out_ref.dtype)
                    below = with_diagonal(tri(packed, packed.T, False), line)
                    out_ref[d, imag] = below.astype(out_ref.dtype)

                @pl.when(side != half)
                def _():
                    other = swap_ref[d].astype(jnp.float32).T.astype(out_ref.dtype)
                    out_ref[d, imag if half else real] = own
                    out_ref[d, real if half else imag] = other

        @pl.when(turn == 1)
        def _():
            for half in range(2):
                real = slice(half * cols, (half + 1) * cols)
                imag = slice((2 + half) * cols, (3 + half) * cols)

                @pl.when(side == half)
                def _():
                    own = folded_ref[d, :cols]
                    other = swap_ref[d].astype(jnp.float32).T.astype(out_ref.dtype)
                    out_ref[d, real] = jnp.where(lower == 1, own, other)
                    out_ref[d, imag] = jnp.where(lower == 1, other, own)

                @pl.when(side != half)
                def _():
                    out_ref[d, real] = folded_ref[d, cols : 2 * cols]
                    out_ref[d, imag] = folded_ref[d, 2 * cols : 3 * cols]

        @pl.when(turn > 1)
        def _():
            out_ref[d, :kept] = folded_ref[d, :kept]

        @pl.when(turn == 2)
        def _():
            out_ref[d, kept:] = two_ref[d]

        @pl.when(turn == 3)
        def _():
            middle = kept + three_ref.shape[1]
            out_ref[d, kept:middle] = three_ref[d]
            out_ref[d, middle:] = last_ref[d]

        return carry

    lax.fori_loop(0, count, each, 0)


def per_device(kernel, place, first, swap, hands, shape, name, step=8):
    devices = first.shape[0]

    def spec(array_shape):
        rest = len(array_shape) - 1
        return pl.BlockSpec((step,) + tuple(array_shape[1:]), lambda i: (i,) + (0,) * rest)

    return pl.pallas_call(
        kernel,
        grid=(devices // step,),
        in_specs=[pl.BlockSpec(memory_space=pltpu.SMEM)]
        + [spec(a.shape) for a in (first, swap, *hands)],
        out_specs=spec(shape),
        out_shape=jax.ShapeDtypeStruct(shape, first.dtype),
        cost_estimate=pl.CostEstimate(
            flops=4 * first.size, bytes_accessed=8 * first.size, transcendentals=0
        ),
        name=name,
    )(place, first, swap, *hands)


def owner_kernel(wave_ref, recv_ref, *refs, sources, groups, cols, fold_in, fold_out):
    out_refs, (held, done) = refs[:-2], refs[-2:]
    out_ref = out_refs[0]
    halves = groups // sources
    rows = halves * cols
    quarter = cols // 4
    kept = 3 * cols + quarter

    def at(block):
        return pl.ds(pl.multiple_of(block * cols, cols), cols)

    def load(d, start):
        return recv_ref[d, start * cols : (start + 1) * cols].astype(jnp.float32)

    def moved(src, col, turn):
        two, three = 2 * cols, 2 * cols + 3 * quarter
        if turn == 2:
            return [(src * groups + col, two, three)]
        return [
            (src * groups + col, three, kept),
            ((src ^ 1) * groups + col, 3 * cols, kept),
        ]

    def load_kept(part, half, src, col, owner_src, turn):
        if part == 0 or half == 0:
            return load(src * groups + col, part * halves + half)
        spans = [(src * groups + col, 3 * cols, kept)] + moved(owner_src, col, turn)
        return jnp.concatenate(
            [recv_ref[d, start:stop].astype(jnp.float32) for d, start, stop in spans], 0
        )

    def put(part, row, col, value):
        held[part, at(row), at(col)] = value.astype(jnp.bfloat16)

    def mirror_whole(src, carry):
        for half in range(halves):
            block = src * halves + half
            for part in range(2):
                for col in range(groups):
                    a = load(src * groups + col, part * halves + half)
                    b = load((col // halves) * groups + block, part * halves + col % halves)
                    put(part, block, col, 0.5 * (a + b.T))
        return carry

    def mirror_folded(src, carry):
        for turn in range(2, sources):
            other = src ^ turn
            for half in range(halves):
                row = src * halves + half
                for side in range(halves):
                    col = other * halves + side
                    for part in range(2):
                        a = load_kept(part, half, src, col, other, turn)
                        b = load_kept(part, side, other, row, src, turn)
                        put(part, row, col, 0.5 * (a + b.T))
        low, high = src * halves, src * halves + 1
        for side in range(halves):
            block = src * halves + side
            d = src * groups + block
            packed = load(d, side)
            line = recv_ref[d, kept:].astype(jnp.float32)[:1]
            put(0, block, block, tri(packed, packed.T, True))
            put(1, block, block, with_diagonal(tri(packed, packed.T, False), line))
        real = load(src * groups + high, 0)
        imag = load(src * groups + low, 1)
        put(0, low, high, real)
        put(0, high, low, real.T)
        put(1, high, low, imag)
        put(1, low, high, imag.T)
        return carry

    def mirror_near(pair, carry):
        low, high = 2 * pair, 2 * pair + 1
        for half in range(halves):
            row, col = low * halves + half, high * halves + half
            real = load(low * groups + col, 0)
            imag = load(high * groups + row, 0)
            put(0, row, col, real)
            put(0, col, row, real.T)
            put(1, col, row, imag)
            put(1, row, col, imag.T)
            col = high * halves + 1 - half
            for part in range(2):
                a = load(low * groups + col, 1 + part)
                b = load(high * groups + row, 1 + part)
                mean = 0.5 * (a + b.T)
                put(part, row, col, mean)
                put(part, col, row, mean.T)
        return carry

    if fold_in:
        lax.fori_loop(0, sources, mirror_folded, 0)
        lax.fori_loop(0, sources // 2, mirror_near, 0)
    else:
        lax.fori_loop(0, sources, mirror_whole, 0)

    wave_real, wave_imag = wave_ref[0], wave_ref[1]
    two_real = wave_real * wave_real - wave_imag * wave_imag
    two_imag = 2.0 * wave_real * wave_imag

    def dot(left, right):
        return jnp.dot(left, right, preferred_element_type=jnp.float32)

    def product(src, carry):
        span = pl.ds(pl.multiple_of(src * rows, rows), rows)
        real, imag = held[0, span, :], held[1, span, :]
        sq_real = dot(real, held[0]) - dot(imag, held[1])
        sq_imag = dot(real, held[1]) + dot(imag, held[0])
        out_real = real.astype(jnp.float32) - (wave_real * sq_real - wave_imag * sq_imag)
        out_imag = imag.astype(jnp.float32) - (wave_real * sq_imag + wave_imag * sq_real)
        left_real, left_imag = sq_real.astype(jnp.bfloat16), sq_imag.astype(jnp.bfloat16)
        cube_real = dot(left_real, held[0]) - dot(left_imag, held[1])
        cube_imag = dot(left_real, held[1]) + dot(left_imag, held[0])
        out_real = (out_real + (two_real * cube_real - two_imag * cube_imag)).astype(jnp.bfloat16)
        out_imag = (out_imag + (two_real * cube_imag + two_imag * cube_real)).astype(jnp.bfloat16)
        if fold_out:
            done[0, span, :] = out_real
            done[1, span, :] = out_imag
        else:
            top = out_refs[0].shape[1] // 2
            for col in range(groups):
                for part, value in enumerate((out_real, out_imag)):
                    tile = value[:, col * cols : (col + 1) * cols]
                    d = src * groups + col
                    out_refs[0][d, part * top : (part + 1) * top] = tile[:top]
                    out_refs[1][d, part * (rows - top) : (part + 1) * (rows - top)] = tile[top:]
        return carry

    lax.fori_loop(0, sources, product, 0)
    if not fold_out:
        return

    def pack(src, carry):
        span = pl.ds(pl.multiple_of(src * rows, rows), rows)
        for turn in range(2, sources):
            other = src ^ turn
            for side in range(halves):
                col = other * halves + side
                d = src * groups + col
                imag = done[1, span, at(col)]
                out_ref[d, :rows] = done[0, span, at(col)]
                out_ref[d, rows:kept] = imag[: kept - rows]
                out_ref[d, kept:] = jnp.zeros((EXTRA, cols), jnp.bfloat16)
                first = kept - rows
                for place, start, stop in moved(other, col, turn):
                    out_ref[place, start:stop] = imag[first : first + stop - start]
                    first += stop - start
        for side in range(halves):
            block = src * halves + side
            d = src * groups + block
            real = done[0, at(block), at(block)].astype(jnp.float32)
            imag = done[1, at(block), at(block)].astype(jnp.float32)
            out_ref[d, side * cols : (side + 1) * cols] = tri(real, imag, True).astype(jnp.bfloat16)
            line = jnp.broadcast_to(diagonal(imag), (EXTRA, cols))
            out_ref[d, kept:] = line.astype(jnp.bfloat16)
        low, high = src * halves, src * halves + 1
        out_ref[src * groups + high, :cols] = done[0, at(low), at(high)]
        out_ref[src * groups + low, cols : 2 * cols] = done[1, at(high), at(low)]
        return carry

    def pack_near(pair, carry):
        low, high = 2 * pair, 2 * pair + 1
        for half in range(halves):
            row, col = low * halves + half, high * halves + half
            out_ref[low * groups + col, :cols] = done[0, at(row), at(col)]
            out_ref[high * groups + row, :cols] = done[1, at(col), at(row)]
            col = high * halves + 1 - half
            for part in range(2):
                slot = slice((1 + part) * cols, (2 + part) * cols)
                out_ref[low * groups + col, slot] = done[part, at(row), at(col)]
                out_ref[high * groups + row, slot] = done[part, at(col), at(row)]
            for d in (low * groups + col, high * groups + row):
                out_ref[d, kept:] = jnp.zeros((EXTRA, cols), jnp.bfloat16)
        return carry

    lax.fori_loop(0, sources, pack, 0)
    lax.fori_loop(0, sources // 2, pack_near, 0)


def owner(wave, recv, sources, groups, fold_in, fold_out):
    if fold_in:
        recv = pltpu.with_memory_space_constraint(recv, pltpu.VMEM)
    devices, _, cols = recv.shape
    total = groups * cols
    whole = 2 * (total // sources)
    lengths = [3 * cols + cols // 4 + EXTRA] if fold_out else [whole - 2 * EDGE, 2 * EDGE]
    return pl.pallas_call(
        functools.partial(
            owner_kernel,
            sources=sources,
            groups=groups,
            cols=cols,
            fold_in=fold_in,
            fold_out=fold_out,
        ),
        in_specs=[
            pl.BlockSpec(memory_space=pltpu.SMEM),
            pl.BlockSpec(memory_space=pltpu.VMEM),
        ],
        out_specs=[pl.BlockSpec(memory_space=pltpu.VMEM)] * len(lengths),
        out_shape=[jax.ShapeDtypeStruct((devices, n, cols), recv.dtype) for n in lengths],
        scratch_shapes=[
            pltpu.VMEM((2, total, total), jnp.bfloat16),
            pltpu.VMEM((2, total, total) if fold_out else (2, 16, 128), jnp.bfloat16),
        ],
        cost_estimate=pl.CostEstimate(
            flops=16 * total**3,
            bytes_accessed=8 * devices * whole * cols,
            transcendentals=0,
        ),
        compiler_params=pltpu.CompilerParams(vmem_limit_bytes=56 << 20),
        name="owned_frequency",
    )(wave, recv)


AXES = ("src", "rcv")


def swap_pairs(sources, groups):
    halves = groups // sources
    pairs = []
    for src in range(sources):
        for side in range(halves):
            here = src * groups + src * halves + side
            pairs.append((here, src * groups + src * halves + 1 - side))
            near = src ^ 1
            pairs.append(
                (near * groups + src * halves + side, src * groups + near * halves + side)
            )
    return pairs


def turn_pairs(sources, groups, start, stop):
    halves = groups // sources
    return [
        ((col // halves ^ start) * groups + col, (col // halves ^ stop) * groups + col)
        for col in range(groups)
    ]


def where_am_i(sources, groups):
    halves = groups // sources
    src, col = lax.axis_index("src"), lax.axis_index("rcv")
    turn, side = src ^ (col // halves), col % halves
    place = jnp.stack([turn, side, (src < col // halves).astype(jnp.int32)])
    return turn, side, place.astype(jnp.int32)


def send_rows(array, start, stop, pairs):
    return lax.ppermute(array[:, start:stop], AXES, pairs)


def fold(spectra, sources, groups):
    devices, length, cols = spectra.shape
    quarter = cols // 4
    kept = 3 * cols + quarter
    turn, side, place = where_am_i(sources, groups)
    diagonal_plane = jnp.where(side == 0, 1, 2)
    near_plane = jnp.where(place[2] == 1, 2 + side, side)
    plane = jnp.where(turn == 0, diagonal_plane, near_plane)
    block = lax.dynamic_slice_in_dim(spectra, plane * cols, cols, 1)
    swap = lax.ppermute(block, AXES, swap_pairs(sources, groups))
    hands = [
        send_rows(spectra, kept, length, turn_pairs(sources, groups, 2, 0)),
        send_rows(spectra, kept, kept + 2 * quarter, turn_pairs(sources, groups, 3, 0)),
        send_rows(spectra, kept + 2 * quarter, length, turn_pairs(sources, groups, 3, 1)),
    ]
    shape = (devices, kept + EXTRA, cols)
    return per_device(fold_kernel, place, spectra, swap, hands, shape, "fold")


def unfold(folded, sources, groups):
    devices, length, cols = folded.shape
    quarter = cols // 4
    kept = 3 * cols + quarter
    middle = 2 * cols + 3 * quarter
    turn, side, place = where_am_i(sources, groups)
    plane = jnp.where(turn == 0, 1 - side, 0)
    block = lax.dynamic_slice_in_dim(folded, plane * cols, cols, 1)
    swap = lax.ppermute(block, AXES, swap_pairs(sources, groups))
    hands = [
        send_rows(folded, 2 * cols, middle, turn_pairs(sources, groups, 0, 2)),
        send_rows(folded, middle, kept, turn_pairs(sources, groups, 0, 3)),
        send_rows(folded, 3 * cols, kept, turn_pairs(sources, groups, 1, 3)),
    ]
    shape = (devices, 4 * cols, cols)
    return per_device(unfold_kernel, place, folded, swap, hands, shape, "unfold")


def exchange(array):
    return lax.all_to_all(array, AXES, 0, 0, tiled=True)


def local_whole(wavefield, inverse_wavelet):
    src_rows, rcv_cols, samples = wavefield.shape
    count_f = inverse_wavelet.shape[1]
    sources, groups = lax.axis_size("src"), lax.axis_size("rcv")
    devices = sources * groups
    me = lax.axis_index(AXES)
    forward, inverse = tables(samples, count_f, F0)
    width = 2 * devices
    wavelets = [
        lax.dynamic_index_in_dim(inverse_wavelet, start + me, 1, keepdims=False)
        for start in range(0, count_f, devices)
    ]

    def spectra(chunk, start, count, step):
        rows = dft(forward[chunk * width : (chunk + 1) * width], wavefield, start, count, step)
        return rows.reshape(devices, 2 * count, rcv_cols)

    plain = exchange(spectra(0, 0, src_rows, src_rows // 2))
    folded = exchange(fold(spectra(1, 0, src_rows, src_rows // 2), sources, groups))
    (cleaned,) = owner(wavelets[0], plain, sources, groups, False, True)
    first = unfold(exchange(cleaned), sources, groups).reshape(width, src_rows, rcv_cols)
    most, rest = owner(wavelets[1], folded, sources, groups, True, False)
    most, rest, first = lax.optimization_barrier((exchange(most), rest, first))
    rest = exchange(rest)
    most = most.reshape(width, src_rows - EDGE, rcv_cols)
    rest = rest.reshape(width, EDGE, rcv_cols)
    out = inverse_rows(inverse, first, most, 0, (src_rows - EDGE) // 2)
    return inverse_rows(inverse, first, rest, src_rows - EDGE, EDGE, out)


def solution(mesh):
    placed = (P("src", "rcv", None), P())

    def local(wavefield, inverse_wavelet):
        sources, groups = lax.axis_size("src"), lax.axis_size("rcv")
        fits = inverse_wavelet.shape[1] == 2 * sources * groups
        if fits and sources == 4 and groups == 2 * sources:
            return local_whole(wavefield, inverse_wavelet)
        return local_sliced(wavefield, inverse_wavelet)

    return jax.shard_map(
        local, mesh=mesh, in_specs=placed, out_specs=P("src", "rcv", None), check_vma=False
    )
```

```python
import functools
import math

import jax
import jax.numpy as jnp
from jax import lax
from jax.experimental import pallas as pl
from jax.experimental.pallas import tpu as pltpu
from jax.sharding import PartitionSpec as P

F0 = 8


def tables(count_t, count_f, first):
    times = jnp.arange(count_t, dtype=jnp.int32)
    freqs = first + jnp.arange(count_f, dtype=jnp.int32)
    phase = freqs[:, None] * times[None, :] % count_t
    angle = phase.astype(jnp.float32) * (2.0 * math.pi / count_t)
    rows = jnp.stack([jnp.cos(angle), -jnp.sin(angle)], 1).reshape(2 * count_f, count_t)
    forward = (rows / math.sqrt(count_t)).astype(jnp.bfloat16)
    inverse = (rows / math.sqrt(count_f)).astype(jnp.bfloat16)
    return (forward, inverse)


def combine(mirror_real, mirror_imag, sq_real, sq_imag, cube_real, cube_imag, wave_real, wave_imag):
    two_real = wave_real * wave_real - wave_imag * wave_imag
    two_imag = 2.0 * wave_real * wave_imag
    out_real = (
        mirror_real
        - (wave_real * sq_real - wave_imag * sq_imag)
        + (two_real * cube_real - two_imag * cube_imag)
    )
    out_imag = (
        mirror_imag
        - (wave_real * sq_imag + wave_imag * sq_real)
        + (two_real * cube_imag + two_imag * cube_real)
    )
    return (out_real, out_imag)


def multiply(left_side, right_side):
    return jnp.einsum("fmk,fkn->fmn", left_side, right_side, preferred_element_type=jnp.float32)


def complex_product(left_side, right_side):
    real_part = multiply(left_side[:, 0], right_side[:, 0]) - multiply(
        left_side[:, 1], right_side[:, 1]
    )
    imag_part = multiply(left_side[:, 0], right_side[:, 1]) + multiply(
        left_side[:, 1], right_side[:, 0]
    )
    return (real_part, imag_part)


def local_sliced(wavefield, inverse_wavelet):
    src_rows, rcv_cols, samples = wavefield.shape
    count_f = inverse_wavelet.shape[1]
    groups = lax.axis_size("rcv")
    per_dev = count_f // groups
    forward, inverse = tables(samples, count_f, F0)
    spectra = jnp.einsum(
        "ct,srt->csr", forward, wavefield, preferred_element_type=jnp.float32
    ).astype(jnp.bfloat16)
    spectra = spectra.reshape(groups, 2 * per_dev, src_rows, rcv_cols)
    slices = lax.all_to_all(spectra, "rcv", split_axis=0, concat_axis=3, tiled=True)
    total_cols = slices.shape[3]
    slices = slices.reshape(per_dev, 2, src_rows, total_cols)
    whole = lax.all_gather(slices, "src", axis=2, tiled=True).astype(jnp.float32)
    all_rows = (0.5 * (whole + jnp.swapaxes(whole, 2, 3))).astype(jnp.bfloat16)
    mirrored = lax.dynamic_slice_in_dim(all_rows, lax.axis_index("src") * src_rows, src_rows, 2)
    sq_real, sq_imag = complex_product(mirrored, all_rows)
    squared = jnp.stack([sq_real, sq_imag], 1).astype(jnp.bfloat16)
    cube_real, cube_imag = complex_product(squared, all_rows)
    wavelet = lax.dynamic_slice_in_dim(inverse_wavelet, lax.axis_index("rcv") * per_dev, per_dev, 1)
    wave_real = wavelet[0][:, None, None]
    wave_imag = wavelet[1][:, None, None]
    out_real, out_imag = combine(
        mirrored[:, 0].astype(jnp.float32),
        mirrored[:, 1].astype(jnp.float32),
        sq_real,
        sq_imag,
        cube_real,
        cube_imag,
        wave_real,
        wave_imag,
    )
    cleaned = (
        jnp.stack([out_real, out_imag], 1)
        .astype(jnp.bfloat16)
        .reshape(1, 2 * per_dev, src_rows, total_cols)
    )
    returned = lax.all_to_all(cleaned, "rcv", split_axis=3, concat_axis=0, tiled=True)
    returned = returned.reshape(2 * count_f, src_rows, rcv_cols)
    return jnp.einsum("csr,ct->srt", returned, inverse, preferred_element_type=jnp.float32).astype(
        jnp.bfloat16
    )


NT_DIMS = (((1,), (1,)), ((), ()))
TN_DIMS = (((0,), (0,)), ((), ()))
EDGE = 16


def dft_kernel(table_ref, wave_ref, out_ref, *, group):
    rows, cols, samples = wave_ref.shape
    for first in range(0, rows, group):
        flat = wave_ref[first : first + group].reshape(group * cols, samples)
        values = lax.dot_general(flat, table_ref[...], NT_DIMS, preferred_element_type=jnp.float32)
        turned = [values[row * cols : (row + 1) * cols].T for row in range(group)]
        stacked = jnp.swapaxes(jnp.stack(turned, 0), 0, 1)
        out_ref[:, first : first + group, :] = stacked.astype(out_ref.dtype)


def dft(table, wave, start, count, step):
    _, cols, samples = wave.shape
    bins = table.shape[0]
    skip = start // step
    return pl.pallas_call(
        functools.partial(dft_kernel, group=16),
        grid=(count // step,),
        in_specs=[
            pl.BlockSpec((bins, samples), lambda i: (0, 0)),
            pl.BlockSpec((step, cols, samples), lambda i: (i + skip, 0, 0)),
        ],
        out_specs=pl.BlockSpec((bins, step, cols), lambda i: (0, i, 0)),
        out_shape=jax.ShapeDtypeStruct((bins, count, cols), jnp.bfloat16),
        cost_estimate=pl.CostEstimate(
            flops=2 * bins * samples * count * cols,
            bytes_accessed=2 * count * cols * (samples + bins),
            transcendentals=0,
        ),
        compiler_params=pltpu.CompilerParams(vmem_limit_bytes=56 << 20),
        name="forward_table",
    )(table, wave)


def inverse_kernel(table_ref, first_ref, last_ref, *refs):
    out_ref = refs[-1]
    table = table_ref[...]
    both = jnp.swapaxes(jnp.concatenate([first_ref[...], last_ref[...]], 0), 0, 1)
    for row in range(out_ref.shape[0]):
        out_ref[row] = lax.dot_general(
            both[row], table, TN_DIMS, preferred_element_type=jnp.float32
        ).astype(out_ref.dtype)


def inverse_rows(table, first, last, start, step, prior=None):
    bins, samples = table.shape
    half, total, cols = first.shape
    count = last.shape[1]
    last_spec = pl.BlockSpec((bins - half, step, cols), lambda i: (0, i, 0))
    if count == step:
        last = pltpu.with_memory_space_constraint(last, pltpu.VMEM)
        last_spec = pl.BlockSpec(memory_space=pltpu.VMEM)
    skip = start // step
    return pl.pallas_call(
        inverse_kernel,
        grid=(count // step,),
        in_specs=[
            pl.BlockSpec((bins, samples), lambda i: (0, 0)),
            pl.BlockSpec((half, step, cols), lambda i: (0, i + skip, 0)),
            last_spec,
        ]
        + ([] if prior is None else [pl.BlockSpec(memory_space=pl.ANY)]),
        out_specs=pl.BlockSpec((step, cols, samples), lambda i: (i + skip, 0, 0)),
        out_shape=jax.ShapeDtypeStruct((total, cols, samples), jnp.bfloat16),
        input_output_aliases={} if prior is None else {3: 0},
        cost_estimate=pl.CostEstimate(
            flops=2 * bins * samples * count * cols,
            bytes_accessed=2 * count * cols * (samples + bins),
            transcendentals=0,
        ),
        compiler_params=pltpu.CompilerParams(vmem_limit_bytes=56 << 20),
        name="inverse_table",
    )(table, first, last, *([] if prior is None else [prior]))


def tri(value, other, upper):
    row = lax.broadcasted_iota(jnp.int32, value.shape, 0)
    col = lax.broadcasted_iota(jnp.int32, value.shape, 1)
    return jnp.where(row <= col, value, other) if upper else jnp.where(row > col, value, other)


def diagonal(value):
    row = lax.broadcasted_iota(jnp.int32, value.shape, 0)
    col = lax.broadcasted_iota(jnp.int32, value.shape, 1)
    return jnp.sum(jnp.where(row == col, value, 0.0), axis=0, keepdims=True)


def with_diagonal(value, line):
    row = lax.broadcasted_iota(jnp.int32, value.shape, 0)
    col = lax.broadcasted_iota(jnp.int32, value.shape, 1)
    return jnp.where(row == col, jnp.broadcast_to(line, value.shape), value)


EXTRA = 8


def fold_kernel(place_ref, whole_ref, swap_ref, two_ref, three_ref, last_ref, out_ref):
    count, length, cols = whole_ref.shape
    kept = out_ref.shape[1] - EXTRA
    turn, side, lower = place_ref[0], place_ref[1], place_ref[2]

    def plane(d, part, half):
        start = (2 * part + half) * cols
        return whole_ref[d, start : start + cols]

    def each(d, carry):
        @pl.when(turn == 0)
        def _():
            for half in range(2):
                real = plane(d, 0, half).astype(jnp.float32)
                imag = plane(d, 1, half).astype(jnp.float32)
                span = slice(half * cols, (half + 1) * cols)

                @pl.when(side == half)
                def _():
                    mean_real = 0.5 * (real + real.T)
                    mean_imag = 0.5 * (imag + imag.T)
                    out_ref[d, span] = tri(mean_real, mean_imag, True).astype(out_ref.dtype)
                    line = jnp.broadcast_to(diagonal(mean_imag), (EXTRA, cols))
                    out_ref[d, kept:] = line.astype(out_ref.dtype)

                @pl.when(side != half)
                def _():
                    own = imag if half else real
                    mean = 0.5 * (own + swap_ref[d].astype(jnp.float32).T)
                    out_ref[d, span] = mean.astype(out_ref.dtype)

            middle = 2 * cols + two_ref.shape[1]
            out_ref[d, 2 * cols : middle] = two_ref[d]
            out_ref[d, middle:kept] = three_ref[d]

        @pl.when(turn == 1)
        def _():
            for half in range(2):

                @pl.when(side == half)
                def _():
                    own = jnp.where(lower == 1, plane(d, 0, half), plane(d, 1, half))
                    mean = 0.5 * (own.astype(jnp.float32) + swap_ref[d].astype(jnp.float32).T)
                    out_ref[d, :cols] = mean.astype(out_ref.dtype)

                @pl.when(side != half)
                def _():
                    out_ref[d, cols : 2 * cols] = plane(d, 0, half)
                    out_ref[d, 2 * cols : 3 * cols] = plane(d, 1, half)

            out_ref[d, 3 * cols : kept] = last_ref[d]
            out_ref[d, kept:] = jnp.zeros((EXTRA, cols), out_ref.dtype)

        @pl.when(turn > 1)
        def _():
            out_ref[d, :kept] = whole_ref[d, :kept]
            out_ref[d, kept:] = jnp.zeros((EXTRA, cols), out_ref.dtype)

        return carry

    lax.fori_loop(0, count, each, 0)


def unfold_kernel(place_ref, folded_ref, swap_ref, two_ref, three_ref, last_ref, out_ref):
    count, length, cols = out_ref.shape
    kept = folded_ref.shape[1] - EXTRA
    turn, side, lower = place_ref[0], place_ref[1], place_ref[2]

    def each(d, carry):
        @pl.when(turn == 0)
        def _():
            for half in range(2):
                own = folded_ref[d, half * cols : (half + 1) * cols]
                real = slice(half * cols, (half + 1) * cols)
                imag = slice((2 + half) * cols, (3 + half) * cols)

                @pl.when(side == half)
                def _():
                    packed = own.astype(jnp.float32)
                    line = folded_ref[d, kept:].astype(jnp.float32)[:1]
                    out_ref[d, real] = tri(packed, packed.T, True).astype(out_ref.dtype)
                    below = with_diagonal(tri(packed, packed.T, False), line)
                    out_ref[d, imag] = below.astype(out_ref.dtype)

                @pl.when(side != half)
                def _():
                    other = swap_ref[d].astype(jnp.float32).T.astype(out_ref.dtype)
                    out_ref[d, imag if half else real] = own
                    out_ref[d, real if half else imag] = other

        @pl.when(turn == 1)
        def _():
            for half in range(2):
                real = slice(half * cols, (half + 1) * cols)
                imag = slice((2 + half) * cols, (3 + half) * cols)

                @pl.when(side == half)
                def _():
                    own = folded_ref[d, :cols]
                    other = swap_ref[d].astype(jnp.float32).T.astype(out_ref.dtype)
                    out_ref[d, real] = jnp.where(lower == 1, own, other)
                    out_ref[d, imag] = jnp.where(lower == 1, other, own)

                @pl.when(side != half)
                def _():
                    out_ref[d, real] = folded_ref[d, cols : 2 * cols]
                    out_ref[d, imag] = folded_ref[d, 2 * cols : 3 * cols]

        @pl.when(turn > 1)
        def _():
            out_ref[d, :kept] = folded_ref[d, :kept]

        @pl.when(turn == 2)
        def _():
            out_ref[d, kept:] = two_ref[d]

        @pl.when(turn == 3)
        def _():
            middle = kept + three_ref.shape[1]
            out_ref[d, kept:middle] = three_ref[d]
            out_ref[d, middle:] = last_ref[d]

        return carry

    lax.fori_loop(0, count, each, 0)


def per_device(kernel, place, first, swap, hands, shape, name, step=8):
    devices = first.shape[0]

    def spec(array_shape):
        rest = len(array_shape) - 1
        return pl.BlockSpec((step,) + tuple(array_shape[1:]), lambda i: (i,) + (0,) * rest)

    return pl.pallas_call(
        kernel,
        grid=(devices // step,),
        in_specs=[pl.BlockSpec(memory_space=pltpu.SMEM)]
        + [spec(a.shape) for a in (first, swap, *hands)],
        out_specs=spec(shape),
        out_shape=jax.ShapeDtypeStruct(shape, first.dtype),
        cost_estimate=pl.CostEstimate(
            flops=4 * first.size, bytes_accessed=8 * first.size, transcendentals=0
        ),
        name=name,
    )(place, first, swap, *hands)


def owner_kernel(wave_ref, recv_ref, *refs, sources, groups, cols, fold_in, fold_out):
    out_refs, (held, done) = refs[:-2], refs[-2:]
    out_ref = out_refs[0]
    halves = groups // sources
    rows = halves * cols
    quarter = cols // 4
    kept = 3 * cols + quarter

    def at(block):
        return pl.ds(pl.multiple_of(block * cols, cols), cols)

    def load(d, start):
        return recv_ref[d, start * cols : (start + 1) * cols].astype(jnp.float32)

    def moved(src, col, turn):
        two, three = 2 * cols, 2 * cols + 3 * quarter
        if turn == 2:
            return [(src * groups + col, two, three)]
        return [
            (src * groups + col, three, kept),
            ((src ^ 1) * groups + col, 3 * cols, kept),
        ]

    def load_kept(part, half, src, col, owner_src, turn):
        if part == 0 or half == 0:
            return load(src * groups + col, part * halves + half)
        spans = [(src * groups + col, 3 * cols, kept)] + moved(owner_src, col, turn)
        return jnp.concatenate(
            [recv_ref[d, start:stop].astype(jnp.float32) for d, start, stop in spans], 0
        )

    def put(part, row, col, value):
        held[part, at(row), at(col)] = value.astype(jnp.bfloat16)

    def mirror_whole(src, carry):
        for half in range(halves):
            block = src * halves + half
            for part in range(2):
                for col in range(groups):
                    a = load(src * groups + col, part * halves + half)
                    b = load((col // halves) * groups + block, part * halves + col % halves)
                    put(part, block, col, 0.5 * (a + b.T))
        return carry

    def mirror_folded(src, carry):
        for turn in range(2, sources):
            other = src ^ turn
            for half in range(halves):
                row = src * halves + half
                for side in range(halves):
                    col = other * halves + side
                    for part in range(2):
                        a = load_kept(part, half, src, col, other, turn)
                        b = load_kept(part, side, other, row, src, turn)
                        put(part, row, col, 0.5 * (a + b.T))
        low, high = src * halves, src * halves + 1
        for side in range(halves):
            block = src * halves + side
            d = src * groups + block
            packed = load(d, side)
            line = recv_ref[d, kept:].astype(jnp.float32)[:1]
            put(0, block, block, tri(packed, packed.T, True))
            put(1, block, block, with_diagonal(tri(packed, packed.T, False), line))
        real = load(src * groups + high, 0)
        imag = load(src * groups + low, 1)
        put(0, low, high, real)
        put(0, high, low, real.T)
        put(1, high, low, imag)
        put(1, low, high, imag.T)
        return carry

    def mirror_near(pair, carry):
        low, high = 2 * pair, 2 * pair + 1
        for half in range(halves):
            row, col = low * halves + half, high * halves + half
            real = load(low * groups + col, 0)
            imag = load(high * groups + row, 0)
            put(0, row, col, real)
            put(0, col, row, real.T)
            put(1, col, row, imag)
            put(1, row, col, imag.T)
            col = high * halves + 1 - half
            for part in range(2):
                a = load(low * groups + col, 1 + part)
                b = load(high * groups + row, 1 + part)
                mean = 0.5 * (a + b.T)
                put(part, row, col, mean)
                put(part, col, row, mean.T)
        return carry

    if fold_in:
        lax.fori_loop(0, sources, mirror_folded, 0)
        lax.fori_loop(0, sources // 2, mirror_near, 0)
    else:
        lax.fori_loop(0, sources, mirror_whole, 0)

    wave_real, wave_imag = wave_ref[0], wave_ref[1]
    two_real = wave_real * wave_real - wave_imag * wave_imag
    two_imag = 2.0 * wave_real * wave_imag

    def dot(left, right):
        return jnp.dot(left, right, preferred_element_type=jnp.float32)

    def product(src, carry):
        span = pl.ds(pl.multiple_of(src * rows, rows), rows)
        real, imag = held[0, span, :], held[1, span, :]
        sq_real = dot(real, held[0]) - dot(imag, held[1])
        sq_imag = dot(real, held[1]) + dot(imag, held[0])
        out_real = real.astype(jnp.float32) - (wave_real * sq_real - wave_imag * sq_imag)
        out_imag = imag.astype(jnp.float32) - (wave_real * sq_imag + wave_imag * sq_real)
        left_real, left_imag = sq_real.astype(jnp.bfloat16), sq_imag.astype(jnp.bfloat16)
        cube_real = dot(left_real, held[0]) - dot(left_imag, held[1])
        cube_imag = dot(left_real, held[1]) + dot(left_imag, held[0])
        out_real = (out_real + (two_real * cube_real - two_imag * cube_imag)).astype(jnp.bfloat16)
        out_imag = (out_imag + (two_real * cube_imag + two_imag * cube_real)).astype(jnp.bfloat16)
        if fold_out:
            done[0, span, :] = out_real
            done[1, span, :] = out_imag
        else:
            top = out_refs[0].shape[1] // 2
            for col in range(groups):
                for part, value in enumerate((out_real, out_imag)):
                    tile = value[:, col * cols : (col + 1) * cols]
                    d = src * groups + col
                    out_refs[0][d, part * top : (part + 1) * top] = tile[:top]
                    out_refs[1][d, part * (rows - top) : (part + 1) * (rows - top)] = tile[top:]
        return carry

    lax.fori_loop(0, sources, product, 0)
    if not fold_out:
        return

    def pack(src, carry):
        span = pl.ds(pl.multiple_of(src * rows, rows), rows)
        for turn in range(2, sources):
            other = src ^ turn
            for side in range(halves):
                col = other * halves + side
                d = src * groups + col
                imag = done[1, span, at(col)]
                out_ref[d, :rows] = done[0, span, at(col)]
                out_ref[d, rows:kept] = imag[: kept - rows]
                out_ref[d, kept:] = jnp.zeros((EXTRA, cols), jnp.bfloat16)
                first = kept - rows
                for place, start, stop in moved(other, col, turn):
                    out_ref[place, start:stop] = imag[first : first + stop - start]
                    first += stop - start
        for side in range(halves):
            block = src * halves + side
            d = src * groups + block
            real = done[0, at(block), at(block)].astype(jnp.float32)
            imag = done[1, at(block), at(block)].astype(jnp.float32)
            out_ref[d, side * cols : (side + 1) * cols] = tri(real, imag, True).astype(jnp.bfloat16)
            line = jnp.broadcast_to(diagonal(imag), (EXTRA, cols))
            out_ref[d, kept:] = line.astype(jnp.bfloat16)
        low, high = src * halves, src * halves + 1
        out_ref[src * groups + high, :cols] = done[0, at(low), at(high)]
        out_ref[src * groups + low, cols : 2 * cols] = done[1, at(high), at(low)]
        return carry

    def pack_near(pair, carry):
        low, high = 2 * pair, 2 * pair + 1
        for half in range(halves):
            row, col = low * halves + half, high * halves + half
            out_ref[low * groups + col, :cols] = done[0, at(row), at(col)]
            out_ref[high * groups + row, :cols] = done[1, at(col), at(row)]
            col = high * halves + 1 - half
            for part in range(2):
                slot = slice((1 + part) * cols, (2 + part) * cols)
                out_ref[low * groups + col, slot] = done[part, at(row), at(col)]
                out_ref[high * groups + row, slot] = done[part, at(col), at(row)]
            for d in (low * groups + col, high * groups + row):
                out_ref[d, kept:] = jnp.zeros((EXTRA, cols), jnp.bfloat16)
        return carry

    lax.fori_loop(0, sources, pack, 0)
    lax.fori_loop(0, sources // 2, pack_near, 0)


def owner(wave, recv, sources, groups, fold_in, fold_out):
    if fold_in:
        recv = pltpu.with_memory_space_constraint(recv, pltpu.VMEM)
    devices, _, cols = recv.shape
    total = groups * cols
    whole = 2 * (total // sources)
    lengths = [3 * cols + cols // 4 + EXTRA] if fold_out else [whole - 2 * EDGE, 2 * EDGE]
    return pl.pallas_call(
        functools.partial(
            owner_kernel,
            sources=sources,
            groups=groups,
            cols=cols,
            fold_in=fold_in,
            fold_out=fold_out,
        ),
        in_specs=[
            pl.BlockSpec(memory_space=pltpu.SMEM),
            pl.BlockSpec(memory_space=pltpu.VMEM),
        ],
        out_specs=[pl.BlockSpec(memory_space=pltpu.VMEM)] * len(lengths),
        out_shape=[jax.ShapeDtypeStruct((devices, n, cols), recv.dtype) for n in lengths],
        scratch_shapes=[
            pltpu.VMEM((2, total, total), jnp.bfloat16),
            pltpu.VMEM((2, total, total) if fold_out else (2, 16, 128), jnp.bfloat16),
        ],
        cost_estimate=pl.CostEstimate(
            flops=16 * total**3,
            bytes_accessed=8 * devices * whole * cols,
            transcendentals=0,
        ),
        compiler_params=pltpu.CompilerParams(vmem_limit_bytes=56 << 20),
        name="owned_frequency",
    )(wave, recv)


AXES = ("src", "rcv")


def swap_pairs(sources, groups):
    halves = groups // sources
    pairs = []
    for src in range(sources):
        for side in range(halves):
            here = src * groups + src * halves + side
            pairs.append((here, src * groups + src * halves + 1 - side))
            near = src ^ 1
            pairs.append(
                (near * groups + src * halves + side, src * groups + near * halves + side)
            )
    return pairs


def turn_pairs(sources, groups, start, stop):
    halves = groups // sources
    return [
        ((col // halves ^ start) * groups + col, (col // halves ^ stop) * groups + col)
        for col in range(groups)
    ]


def where_am_i(sources, groups):
    halves = groups // sources
    src, col = lax.axis_index("src"), lax.axis_index("rcv")
    turn, side = src ^ (col // halves), col % halves
    place = jnp.stack([turn, side, (src < col // halves).astype(jnp.int32)])
    return turn, side, place.astype(jnp.int32)


def send_rows(array, start, stop, pairs):
    return lax.ppermute(array[:, start:stop], AXES, pairs)


def fold(spectra, sources, groups):
    devices, length, cols = spectra.shape
    quarter = cols // 4
    kept = 3 * cols + quarter
    turn, side, place = where_am_i(sources, groups)
    diagonal_plane = jnp.where(side == 0, 1, 2)
    near_plane = jnp.where(place[2] == 1, 2 + side, side)
    plane = jnp.where(turn == 0, diagonal_plane, near_plane)
    block = lax.dynamic_slice_in_dim(spectra, plane * cols, cols, 1)
    swap = lax.ppermute(block, AXES, swap_pairs(sources, groups))
    hands = [
        send_rows(spectra, kept, length, turn_pairs(sources, groups, 2, 0)),
        send_rows(spectra, kept, kept + 2 * quarter, turn_pairs(sources, groups, 3, 0)),
        send_rows(spectra, kept + 2 * quarter, length, turn_pairs(sources, groups, 3, 1)),
    ]
    shape = (devices, kept + EXTRA, cols)
    return per_device(fold_kernel, place, spectra, swap, hands, shape, "fold")


def unfold(folded, sources, groups):
    devices, length, cols = folded.shape
    quarter = cols // 4
    kept = 3 * cols + quarter
    middle = 2 * cols + 3 * quarter
    turn, side, place = where_am_i(sources, groups)
    plane = jnp.where(turn == 0, 1 - side, 0)
    block = lax.dynamic_slice_in_dim(folded, plane * cols, cols, 1)
    swap = lax.ppermute(block, AXES, swap_pairs(sources, groups))
    hands = [
        send_rows(folded, 2 * cols, middle, turn_pairs(sources, groups, 0, 2)),
        send_rows(folded, middle, kept, turn_pairs(sources, groups, 0, 3)),
        send_rows(folded, 3 * cols, kept, turn_pairs(sources, groups, 1, 3)),
    ]
    shape = (devices, 4 * cols, cols)
    return per_device(unfold_kernel, place, folded, swap, hands, shape, "unfold")


def exchange(array):
    return lax.all_to_all(array, AXES, 0, 0, tiled=True)


def local_whole(wavefield, inverse_wavelet):
    src_rows, rcv_cols, samples = wavefield.shape
    count_f = inverse_wavelet.shape[1]
    sources, groups = lax.axis_size("src"), lax.axis_size("rcv")
    devices = sources * groups
    me = lax.axis_index(AXES)
    forward, inverse = tables(samples, count_f, F0)
    width = 2 * devices
    wavelets = [
        lax.dynamic_index_in_dim(inverse_wavelet, start + me, 1, keepdims=False)
        for start in range(0, count_f, devices)
    ]

    def spectra(chunk, start, count, step):
        rows = dft(forward[chunk * width : (chunk + 1) * width], wavefield, start, count, step)
        return rows.reshape(devices, 2 * count, rcv_cols)

    plain = exchange(spectra(0, 0, src_rows, src_rows // 2))
    folded = exchange(fold(spectra(1, 0, src_rows, src_rows // 2), sources, groups))
    (cleaned,) = owner(wavelets[0], plain, sources, groups, False, True)
    first = unfold(exchange(cleaned), sources, groups).reshape(width, src_rows, rcv_cols)
    most, rest = owner(wavelets[1], folded, sources, groups, True, False)
    most, rest, first = lax.optimization_barrier((exchange(most), rest, first))
    rest = exchange(rest)
    most = most.reshape(width, src_rows - EDGE, rcv_cols)
    rest = rest.reshape(width, EDGE, rcv_cols)
    out = inverse_rows(inverse, first, most, 0, (src_rows - EDGE) // 2)
    return inverse_rows(inverse, first, rest, src_rows - EDGE, EDGE, out)


def solution(mesh):
    placed = (P("src", "rcv", None), P())

    def local(wavefield, inverse_wavelet):
        sources, groups = lax.axis_size("src"), lax.axis_size("rcv")
        fits = inverse_wavelet.shape[1] == 2 * sources * groups
        if fits and sources == 4 and groups == 2 * sources:
            return local_whole(wavefield, inverse_wavelet)
        return local_sliced(wavefield, inverse_wavelet)

    return jax.shard_map(
        local, mesh=mesh, in_specs=placed, out_specs=P("src", "rcv", None), check_vma=False
    )
```
